32 devices in a mesh: group: 2 (over y), seq: 4 (over z), head: 2 (over x), rep: 2 (over core).
Axes of the slice: x: 2, y: 2, z: 4, core: 2. Of those that a mesh axis runs over, the one named last changes fastest.
Arguments:
- span_q: bfloat16 [8, 128, 8192], P('group', 'seq', ('head', 'rep')), parts along dimension 0, may hold values from -144 to 144
- span_raw_keys: bfloat16 [8, 128, 1024], P('group', 'seq', 'head'), parts along dimension 0, may hold values from -6 to 6
- span_raw_values: bfloat16 [8, 128, 1024], P('group', 'seq', 'head'), parts along dimension 0, may hold values from -6 to 6
- prompt_cache_keys: bfloat16 [8, 256, 1024], P('group', 'seq', 'head'), parts along dimension 0, may hold values from -6 to 6
- prompt_cache_values: bfloat16 [8, 256, 1024], P('group', 'seq', 'head'), parts along dimension 0, may hold values from -6 to 6
- span_offsets: int32 [8], P('group'), parts along dimension 0, may hold values from 1 to 256
- decode_new_queries: bfloat16 [64, 4, 8192], P(('group', 'seq'), None, ('head', 'rep')), parts along dimension 0, may hold values from -144 to 144
- decode_new_keys: bfloat16 [64, 4, 1024], P(('group', 'seq'), None, 'head'), parts along dimension 0, may hold values from -6 to 6
- decode_new_values: bfloat16 [64, 4, 1024], P(('group', 'seq'), None, 'head'), parts along dimension 0, may hold values from -6 to 6
- generated_keys: bfloat16 [64, 128, 1024], P(('group', 'seq'), None, 'head'), parts along dimension 0, may hold values from -6 to 6
- generated_values: bfloat16 [64, 128, 1024], P(('group', 'seq'), None, 'head'), parts along dimension 0, may hold values from -6 to 6
- row_request: int32 [64], P(('group', 'seq')), parts along dimension 0, may hold values from 0 to 3
- row_length: int32 [64], P(('group', 'seq')), parts along dimension 0, may hold values from 1 to 128
Outputs:
- span_output: bfloat16 [8, 128, 8192], P('group', 'seq', ('head', 'rep')), parts along dimension 0
- dec_out: bfloat16 [64, 4, 8192], P(('group', 'seq'), None, ('head', 'rep')), parts along dimension 0
The draws below stay inside these ranges and needn't reach their ends.
There are 2 independent parts, one for each index of `group`. The reference program is written for one: setup_inputs(seed, part) draws one part's arguments, and reference() takes and returns one part's arrays. A program takes and returns all parts, laid end to end along the dimension named above; each array names one. Nothing has to cross between parts.
All inputs are finite; a program needn't handle non-finite values.
Results may differ from the reference program's by a relative error of at most 0.012.
Values may be sent and summed in bfloat16 or wider, within the bound.
No kernel may reach another device: no remote copies, remote signals or barrier semaphores. Data moves between devices by JAX's collectives and lax.ppermute only.
A program may use at most 64 MiB of HBM per device.

```python
import math
import jax
import jax.numpy as jnp
from jax import lax

QUERY_HEADS = 64
KEY_VALUE_HEADS = 8
HEAD_WIDTH = 128
PROMPT_COUNT = 4
DECODE_STEPS = 4
GENERATED_SLOTS = 128
SPAN_TOKENS = 128
PROMPT_SLOTS = 256
DECODE_ROWS = 32


def scaled_queries(key, shape):
    first_key, second_key = jax.random.split(key, 2)
    heads_shape = shape[:-1] + (QUERY_HEADS, HEAD_WIDTH)
    lead = shape[:-1] + (QUERY_HEADS, 1)
    base = jnp.clip(jax.random.normal(first_key, heads_shape, jnp.float32), -6.0, 6.0)
    scales = jnp.exp(jax.random.uniform(second_key, lead, jnp.float32, math.log(0.3), math.log(3.0)))
    return (base * scales).reshape(shape)


def draw_span_q(key, part):
    return scaled_queries(jax.random.fold_in(key, 11), (PROMPT_COUNT, SPAN_TOKENS, QUERY_HEADS * HEAD_WIDTH)).astype(jnp.bfloat16)


def draw_decode_new_queries(key, part):
    return scaled_queries(jax.random.fold_in(key, 23), (DECODE_ROWS, DECODE_STEPS, QUERY_HEADS * HEAD_WIDTH)).astype(jnp.bfloat16)


def set_ends(drawn, rng, low, high):
    spot = [jax.random.randint(jax.random.fold_in(rng, axis), (), 0, length) for axis, length in enumerate(drawn.shape)]
    longest = drawn.shape.index(max(drawn.shape))
    next_to = spot[:longest] + [(spot[longest] + 1) % drawn.shape[longest]] + spot[longest + 1:]
    return drawn.at[tuple(spot)].set(low).at[tuple(next_to)].set(high)


def steps_of(own_key, extent, shards, smallest, top_value):
    def one(dim, parts):
        heights = jax.random.uniform(jax.random.fold_in(jax.random.fold_in(own_key, 6), dim), (parts,), jnp.float32, smallest / len(shards), top_value / len(shards))
        return jnp.repeat(jnp.exp(heights), extent[dim] // parts).reshape((-1,) + (1,) * (len(extent) - dim - 1))

    loudness = one(*shards[0])
    for cut in shards[1:]:
        loudness = loudness * one(*cut)
    return loudness


def scatter_about(key, dims, scale, most, cuts=(), kind=jnp.bfloat16):
    loudness = steps_of(key, dims, cuts, -0.22, 0.18) if cuts else 1.0
    drawn = jax.random.normal(key, dims, jnp.float32) * scale * loudness
    return jnp.minimum(jnp.maximum(drawn, -most), most).astype(kind)


def setup_inputs(seed: int = 0, part: int = 0) -> dict:
    streams_of = jax.random.split(jax.random.key(seed), 14)
    part_keys = jax.random.split(jax.random.fold_in(streams_of[13], part), 14)
    return {
        "span_q": draw_span_q(jax.random.fold_in(jax.random.fold_in(streams_of[13], part), 71), part),
        "span_raw_keys": scatter_about(part_keys[1], (PROMPT_COUNT, SPAN_TOKENS, KEY_VALUE_HEADS * HEAD_WIDTH), 1.0, 6.0, ((1, 4), (2, 2))),
        "span_raw_values": scatter_about(part_keys[2], (PROMPT_COUNT, SPAN_TOKENS, KEY_VALUE_HEADS * HEAD_WIDTH), 1.0, 6.0, ((1, 4), (2, 2))),
        "prompt_cache_keys": scatter_about(part_keys[3], (PROMPT_COUNT, PROMPT_SLOTS, KEY_VALUE_HEADS * HEAD_WIDTH), 1.0, 6.0, ((1, 4), (2, 2))),
        "prompt_cache_values": scatter_about(part_keys[4], (PROMPT_COUNT, PROMPT_SLOTS, KEY_VALUE_HEADS * HEAD_WIDTH), 1.0, 6.0, ((1, 4), (2, 2))),
        "span_offsets": set_ends(jax.random.randint(part_keys[5], (PROMPT_COUNT,), 1, PROMPT_SLOTS + 1), jax.random.fold_in(part_keys[5], 1), 1, PROMPT_SLOTS).astype(jnp.int32),
        "decode_new_queries": draw_decode_new_queries(jax.random.fold_in(jax.random.fold_in(streams_of[13], part), 71), part),
        "decode_new_keys": scatter_about(part_keys[7], (DECODE_ROWS, DECODE_STEPS, KEY_VALUE_HEADS * HEAD_WIDTH), 1.0, 6.0, ((0, 4), (2, 2))),
        "decode_new_values": scatter_about(part_keys[8], (DECODE_ROWS, DECODE_STEPS, KEY_VALUE_HEADS * HEAD_WIDTH), 1.0, 6.0, ((0, 4), (2, 2))),
        "generated_keys": scatter_about(part_keys[9], (DECODE_ROWS, GENERATED_SLOTS, KEY_VALUE_HEADS * HEAD_WIDTH), 1.0, 6.0, ((0, 4), (2, 2))),
        "generated_values": scatter_about(part_keys[10], (DECODE_ROWS, GENERATED_SLOTS, KEY_VALUE_HEADS * HEAD_WIDTH), 1.0, 6.0, ((0, 4), (2, 2))),
        "row_request": set_ends(jax.random.randint(part_keys[11], (DECODE_ROWS,), 0, PROMPT_COUNT), jax.random.fold_in(part_keys[11], 1), 0, PROMPT_COUNT - 1).astype(jnp.int32),
        "row_length": set_ends(jax.random.randint(part_keys[12], (DECODE_ROWS,), 1, GENERATED_SLOTS + 1), jax.random.fold_in(part_keys[12], 1), 1, GENERATED_SLOTS).astype(jnp.int32),
    }


very_low = -1.0e30


def apply_rotary(values, positions):
    width = values.shape[-1]
    half = width // 2
    freqs = jnp.exp(jnp.arange(half, dtype=jnp.float32) * (-2.0 * math.log(500000.0) / width))
    angles = positions.astype(jnp.float32)[..., None] * freqs
    cosine = jnp.cos(angles)
    sine = jnp.sin(angles)
    first = values[..., :half]
    second = values[..., half:]
    return jnp.concatenate([first * cosine - second * sine, second * cosine + first * sine], axis=-1)


def attend(queries, keys, values, mask, scale):
    scores = jnp.dot(queries, keys.T, preferred_element_type=jnp.float32) * scale
    scores = jnp.where(mask, scores, very_low)
    peak = jnp.max(scores, axis=-1, keepdims=True)
    weights = jnp.where(mask, jnp.exp(scores - peak), 0.0)
    summed = jnp.dot(weights.astype(jnp.bfloat16), values, preferred_element_type=jnp.float32)
    return summed / jnp.sum(weights, axis=-1, keepdims=True)


def reference(span_q, span_raw_keys, span_raw_values, prompt_cache_keys, prompt_cache_values, span_offsets, decode_new_queries, decode_new_keys, decode_new_values, generated_keys, generated_values, row_request, row_length):
    query_groups = QUERY_HEADS // KEY_VALUE_HEADS
    scale = HEAD_WIDTH ** -0.5
    token_index = jnp.arange(SPAN_TOKENS, dtype=jnp.int32)
    span_positions = span_offsets[:, None] + token_index[None, :]
    span_query_rows = apply_rotary(span_q.astype(jnp.float32).reshape(PROMPT_COUNT, SPAN_TOKENS, QUERY_HEADS, HEAD_WIDTH), span_positions[:, :, None]).astype(jnp.bfloat16)
    span_keys_rotated = apply_rotary(span_raw_keys.astype(jnp.float32).reshape(PROMPT_COUNT, SPAN_TOKENS, KEY_VALUE_HEADS, HEAD_WIDTH), span_positions[:, :, None]).astype(jnp.bfloat16)
    element_queries = span_query_rows.reshape(PROMPT_COUNT, SPAN_TOKENS, KEY_VALUE_HEADS, query_groups, HEAD_WIDTH).transpose(0, 2, 1, 3, 4).reshape(PROMPT_COUNT * KEY_VALUE_HEADS, SPAN_TOKENS * query_groups, HEAD_WIDTH)
    element_keys = jnp.concatenate([prompt_cache_keys.reshape(PROMPT_COUNT, PROMPT_SLOTS, KEY_VALUE_HEADS, HEAD_WIDTH), span_keys_rotated], axis=1).transpose(0, 2, 1, 3).reshape(PROMPT_COUNT * KEY_VALUE_HEADS, PROMPT_SLOTS + SPAN_TOKENS, HEAD_WIDTH)
    element_values = jnp.concatenate([prompt_cache_values.reshape(PROMPT_COUNT, PROMPT_SLOTS, KEY_VALUE_HEADS, HEAD_WIDTH), span_raw_values.reshape(PROMPT_COUNT, SPAN_TOKENS, KEY_VALUE_HEADS, HEAD_WIDTH)], axis=1).transpose(0, 2, 1, 3).reshape(PROMPT_COUNT * KEY_VALUE_HEADS, PROMPT_SLOTS + SPAN_TOKENS, HEAD_WIDTH)
    element_begin = jnp.repeat(span_offsets, KEY_VALUE_HEADS)
    slot_index = jnp.arange(PROMPT_SLOTS + SPAN_TOKENS, dtype=jnp.int32)
    row_token = jnp.arange(SPAN_TOKENS * query_groups, dtype=jnp.int32) // query_groups

    def one_item(items):
        queries, keys, values, begin = items
        in_prefix = (slot_index[None, :] < PROMPT_SLOTS) & (slot_index[None, :] < begin)
        in_span = (slot_index[None, :] >= PROMPT_SLOTS) & (slot_index[None, :] - PROMPT_SLOTS <= row_token[:, None])
        return attend(queries, keys, values, in_prefix | in_span, scale)

    prefill_attention = lax.map(one_item, (element_queries, element_keys, element_values, element_begin))
    span_output = prefill_attention.reshape(PROMPT_COUNT, KEY_VALUE_HEADS, SPAN_TOKENS, query_groups, HEAD_WIDTH).transpose(0, 2, 1, 3, 4).reshape(PROMPT_COUNT, SPAN_TOKENS, QUERY_HEADS * HEAD_WIDTH).astype(jnp.bfloat16)

    decode_positions = span_offsets[row_request][:, None] + SPAN_TOKENS + row_length[:, None] + jnp.arange(DECODE_STEPS, dtype=jnp.int32)[None, :]
    decode_query_rows = apply_rotary(decode_new_queries.astype(jnp.float32).reshape(DECODE_ROWS, DECODE_STEPS, QUERY_HEADS, HEAD_WIDTH), decode_positions[:, :, None]).astype(jnp.bfloat16).reshape(DECODE_ROWS, DECODE_STEPS, KEY_VALUE_HEADS, query_groups, HEAD_WIDTH)
    fresh_keys = apply_rotary(decode_new_keys.astype(jnp.float32).reshape(DECODE_ROWS, DECODE_STEPS, KEY_VALUE_HEADS, HEAD_WIDTH), decode_positions[:, :, None]).astype(jnp.bfloat16)
    fresh_values = decode_new_values.reshape(DECODE_ROWS, DECODE_STEPS, KEY_VALUE_HEADS, HEAD_WIDTH)
    step_row = jnp.arange(DECODE_STEPS * query_groups, dtype=jnp.int32) // query_groups
    prefix_slots = jnp.arange(PROMPT_SLOTS, dtype=jnp.int32)
    gen_slots = jnp.arange(GENERATED_SLOTS, dtype=jnp.int32)
    step_slots = jnp.arange(DECODE_STEPS, dtype=jnp.int32)

    def one_row(items):
        queries, keys_new, values_new, generated_key_rows, generated_value_rows, prompt_number, length = items
        begin = span_offsets[prompt_number]
        prompt_keys = prompt_cache_keys[prompt_number].reshape(PROMPT_SLOTS, KEY_VALUE_HEADS, HEAD_WIDTH)
        prompt_values = prompt_cache_values[prompt_number].reshape(PROMPT_SLOTS, KEY_VALUE_HEADS, HEAD_WIDTH)
        keys_span = span_keys_rotated[prompt_number]
        span_value_rows = span_raw_values[prompt_number].reshape(SPAN_TOKENS, KEY_VALUE_HEADS, HEAD_WIDTH)
        generated_key_rows = generated_key_rows.reshape(GENERATED_SLOTS, KEY_VALUE_HEADS, HEAD_WIDTH)
        generated_value_rows = generated_value_rows.reshape(GENERATED_SLOTS, KEY_VALUE_HEADS, HEAD_WIDTH)
        rows_here = DECODE_STEPS * query_groups
        mask = jnp.concatenate([
            jnp.broadcast_to((prefix_slots < begin)[None, :], (rows_here, PROMPT_SLOTS)),
            jnp.ones((rows_here, SPAN_TOKENS), dtype=bool),
            jnp.broadcast_to((gen_slots < length)[None, :], (rows_here, GENERATED_SLOTS)),
            step_slots[None, :] <= step_row[:, None]], axis=1)
        outputs = []
        for head_number in range(KEY_VALUE_HEADS):
            keys_all = jnp.concatenate([prompt_keys[:, head_number], keys_span[:, head_number], generated_key_rows[:, head_number], keys_new[:, head_number]], axis=0)
            values_all = jnp.concatenate([prompt_values[:, head_number], span_value_rows[:, head_number], generated_value_rows[:, head_number], values_new[:, head_number]], axis=0)
            query = queries[:, head_number].reshape(rows_here, HEAD_WIDTH)
            outputs.append(attend(query, keys_all, values_all, mask, scale).reshape(DECODE_STEPS, 1, query_groups, HEAD_WIDTH))
        return jnp.concatenate(outputs, axis=1).reshape(DECODE_STEPS, QUERY_HEADS * HEAD_WIDTH)

    decoded = lax.map(one_row, (decode_query_rows, fresh_keys, fresh_values, generated_keys, generated_values, row_request, row_length))
    return span_output, decoded.astype(jnp.bfloat16)
```

```python
import functools
import math

import jax
import jax.numpy as jnp
from jax import lax
from jax.experimental import pallas as pl
from jax.experimental.pallas import tpu as pltpu
from jax.sharding import PartitionSpec as P

QUERY_HEADS = 64
KEY_VALUE_HEADS = 8
HEAD_WIDTH = 128

very_low = -1e30
ANY = pl.BlockSpec(memory_space=pl.ANY)
SMEM = pl.BlockSpec(memory_space=pltpu.SMEM)
VMEM = pl.BlockSpec(memory_space=pltpu.VMEM)


def rotary_tables(positions):
    width = HEAD_WIDTH
    half = width // 2
    lane = jnp.arange(width, dtype=jnp.int32)
    index = lane % half
    freqs = jnp.exp(index.astype(jnp.float32) * (-2.0 * math.log(500000.0) / width))
    angles = positions.astype(jnp.float32)[..., None] * freqs
    sine = jnp.sin(angles)
    return jnp.cos(angles), jnp.where(lane < half, -sine, sine)


def rotate(x, cosine, sine):
    return x * cosine + pltpu.roll(x, HEAD_WIDTH // 2, axis=x.ndim - 1) * sine


def first_head(q_heads, kv_local):
    groups = QUERY_HEADS // KEY_VALUE_HEADS
    head = lax.axis_index("head")
    block = head * lax.axis_size("rep") + lax.axis_index("rep")
    return block * q_heads // groups - head * kv_local


def dot_nt(a, b):
    return lax.dot_general(a, b, (((1,), (1,)), ((), ())), preferred_element_type=jnp.float32)


def pack_kernel(q_heads, kv_local, used, *refs):
    ins, outs, sem = refs[:4], refs[4:-1], refs[-1]
    width = used * HEAD_WIDTH
    pre = ins[0].shape[1]
    ch = ins[2].shape[1]
    lanes = pl.ds(pl.multiple_of(first_head(q_heads, kv_local) * HEAD_WIDTH, HEAD_WIDTH), width)
    copies = []
    for p, out in enumerate(outs):
        for j, ref in enumerate(ins):
            rows = pl.ds(0, pre) if j < 2 else pl.ds(pre, ch)
            copies.append(
                pltpu.make_async_copy(
                    ref.at[p, :, lanes], out.at[j % 2, rows, :], sem.at[p, j]
                )
            )
    for copy in copies:
        copy.start()
    for copy in copies:
        copy.wait()


def query_kernel(used, per_kv, q_ref, cos_ref, sin_ref, out_ref):
    cosine = cos_ref[0]
    sine = sin_ref[0]
    ch = cosine.shape[0]
    for h in range(used):
        for g in range(per_kv):
            lanes = pl.ds((h * per_kv + g) * HEAD_WIDTH, HEAD_WIDTH)
            x = q_ref[0, :, lanes].astype(jnp.float32)
            out_ref[0, h, pl.ds(g * ch, ch), :] = rotate(x, cosine, sine).astype(jnp.bfloat16)


def decode_kernel(
    used,
    per_kv,
    rows_step,
    length_ref,
    q_ref,
    cos_ref,
    sin_ref,
    gk_ref,
    gv_ref,
    nk_ref,
    nv_ref,
    dq_ref,
    acc_ref,
    top_ref,
    total_ref,
    q_scr,
    k_scr,
    v_scr,
):
    scale = HEAD_WIDTH ** (-0.5)
    steps = q_ref.shape[1]
    gen = gk_ref.shape[1]
    step_rows = per_kv * steps
    pad = k_scr.shape[2]
    base = pl.program_id(0) * rows_step
    k_scr[...] = jnp.zeros_like(k_scr)
    v_scr[...] = jnp.zeros_like(v_scr)
    column = lax.broadcasted_iota(jnp.int32, (step_rows, gen + pad), 1)
    step = lax.broadcasted_iota(jnp.int32, (step_rows, gen + pad), 0) % steps
    new_seen = (column >= gen) & (column - gen <= step)
    for r in range(rows_step):
        cosine = cos_ref[r]
        sine = sin_ref[r]
        seen = (column < length_ref[base + r]) | new_seen
        for h in range(used):
            for g in range(per_kv):
                lanes = pl.ds((h * per_kv + g) * HEAD_WIDTH, HEAD_WIDTH)
                x = q_ref[r, :, lanes].astype(jnp.float32)
                q_scr[r, h, pl.ds(g * steps, steps), :] = rotate(x, cosine, sine)
            lanes = pl.ds(h * HEAD_WIDTH, HEAD_WIDTH)
            k_scr[r, h, pl.ds(0, steps), :] = rotate(
                nk_ref[r, :, lanes].astype(jnp.float32), cosine, sine
            )
            v_scr[r, h, pl.ds(0, steps), :] = nv_ref[r, :, lanes].astype(jnp.float32)
            queries = q_scr[r, h].astype(jnp.bfloat16)
            keys = jnp.concatenate([gk_ref[r, :, lanes], k_scr[r, h].astype(jnp.bfloat16)], axis=0)
            values = jnp.concatenate(
                [gv_ref[r, :, lanes], v_scr[r, h].astype(jnp.bfloat16)], axis=0
            )
            scores = jnp.where(seen, dot_nt(queries, keys) * scale, very_low)
            top = jnp.max(scores, axis=1, keepdims=True)
            weights = jnp.exp(scores - top)
            total = jnp.sum(weights, axis=1, keepdims=True)
            rows = pl.ds(r * step_rows, step_rows)
            dq_ref[h, rows, :] = queries
            acc_ref[h, rows, :] = jnp.dot(
                weights.astype(jnp.bfloat16), values, preferred_element_type=jnp.float32
            )
            top_ref[h, rows, :] = jnp.broadcast_to(top, (step_rows, HEAD_WIDTH))
            total_ref[h, rows, :] = jnp.broadcast_to(total, (step_rows, HEAD_WIDTH))


def stage_kernel(p, used, per_kv, steps, *refs):
    shards = lax.axis_size("seq")
    begin_ref, request_ref = refs[:2]
    chunks = refs[2 : 2 + shards]
    cos_ref, sin_ref, q_ref, dq_ref, acc_ref, top_ref, total_ref = refs[2 + shards : 9 + shards]
    span_ref, dec_ref, k_scr, v_scr, d_scr, sem = refs[-6:]
    scale = HEAD_WIDTH ** (-0.5)
    me = lax.axis_index("seq")
    ch = span_ref.shape[1]
    pre = chunks[0].shape[1] - ch
    prefix = pre * shards
    rows_local = request_ref.shape[0]
    step_rows = per_kv * steps
    begin = begin_ref[p]
    for k, chunk in enumerate(chunks):
        shard = lax.rem(me + shards - k, shards)
        pre_rows = pl.ds(pl.multiple_of(shard * pre, pre), pre)
        ch_rows = pl.ds(pl.multiple_of(prefix + shard * ch, ch), ch)
        tokens = pl.ds(pl.multiple_of(shard * ch, ch), ch)
        cosine = cos_ref[0, tokens, :]
        sine = sin_ref[0, tokens, :]
        k_scr[pre_rows, :] = chunk[0, pl.ds(0, pre), :]
        v_scr[pre_rows, :] = chunk[1, pl.ds(0, pre), :]
        v_scr[ch_rows, :] = chunk[1, pl.ds(pre, ch), :]
        for h in range(used):
            lanes = pl.ds(h * HEAD_WIDTH, HEAD_WIDTH)
            x = chunk[0, pl.ds(pre, ch), lanes].astype(jnp.float32)
            k_scr[ch_rows, lanes] = rotate(x, cosine, sine).astype(jnp.bfloat16)

    keys_all = k_scr.shape[0]
    rows = q_ref.shape[2]
    column = lax.broadcasted_iota(jnp.int32, (rows, keys_all), 1)
    token = lax.broadcasted_iota(jnp.int32, (rows, keys_all), 0) % ch + me * ch
    limit = jnp.where(column < prefix, begin, token + (prefix + 1))
    seen = column < limit
    dec_rows = dq_ref.shape[1]
    dec_column = lax.broadcasted_iota(jnp.int32, (dec_rows, keys_all), 1)
    dec_seen = (dec_column < begin) | (dec_column >= prefix)
    for h in range(used):
        lanes = pl.ds(h * HEAD_WIDTH, HEAD_WIDTH)
        keys = k_scr[:, lanes]
        values = v_scr[:, lanes]
        scores = jnp.where(seen, dot_nt(q_ref[0, h], keys) * scale, very_low)
        top = jnp.max(scores, axis=1, keepdims=True)
        weights = jnp.exp(scores - top)
        total = jnp.sum(weights, axis=1, keepdims=True)
        out = jnp.dot(weights.astype(jnp.bfloat16), values, preferred_element_type=jnp.float32)
        out = (out / total).astype(jnp.bfloat16)
        for g in range(per_kv):
            span_ref[0, :, pl.ds((h * per_kv + g) * HEAD_WIDTH, HEAD_WIDTH)] = out[
                g * ch : (g + 1) * ch
            ]

        scores = jnp.where(dec_seen, dot_nt(dq_ref[h], keys) * scale, very_low)
        old_top = top_ref[h][:, :1]
        top = jnp.maximum(jnp.max(scores, axis=1, keepdims=True), old_top)
        weights = jnp.exp(scores - top)
        factor = jnp.exp(old_top - top)
        total = jnp.sum(weights, axis=1, keepdims=True) + total_ref[h][:, :1] * factor
        out = (
            jnp.dot(weights.astype(jnp.bfloat16), values, preferred_element_type=jnp.float32)
            + acc_ref[h] * factor
        )
        out = out / total
        for r in range(rows_local):
            @pl.when(request_ref[r] == p)
            def _():
                for g in range(per_kv):
                    start = r * step_rows + g * steps
                    d_scr[r, :, pl.ds((h * per_kv + g) * HEAD_WIDTH, HEAD_WIDTH)] = out[
                        start : start + steps
                    ].astype(jnp.bfloat16)

    for r in range(rows_local):
        @pl.when(request_ref[r] == p)
        def _():
            pltpu.make_async_copy(d_scr.at[r], dec_ref.at[r], sem.at[r]).start()

    for r in range(rows_local):
        @pl.when(request_ref[r] == p)
        def _():
            pltpu.make_async_copy(d_scr.at[r], dec_ref.at[r], sem.at[r]).wait()


def body(
    span_q,
    span_raw_keys,
    span_raw_values,
    prompt_cache_keys,
    prompt_cache_values,
    span_offsets,
    decode_new_queries,
    decode_new_keys,
    decode_new_values,
    generated_keys,
    generated_values,
    row_request,
    row_length,
):
    prompts, ch, q_width = span_q.shape
    pre = prompt_cache_keys.shape[1]
    groups = QUERY_HEADS // KEY_VALUE_HEADS
    q_heads = q_width // HEAD_WIDTH
    kv_local = span_raw_keys.shape[2] // HEAD_WIDTH
    used = max(1, q_heads // groups)
    per_kv = q_heads // used
    width = used * HEAD_WIDTH
    shards = lax.axis_size("seq")
    rows_local, steps = decode_new_queries.shape[:2]
    gen = generated_keys.shape[1]
    step_rows = per_kv * steps
    bf16 = jnp.bfloat16
    f32 = jnp.float32
    params = functools.partial(pltpu.CompilerParams, vmem_limit_bytes=24 << 20)

    own = pl.pallas_call(
        functools.partial(pack_kernel, q_heads, kv_local, used),
        out_shape=[jax.ShapeDtypeStruct((2, pre + ch, width), bf16)] * prompts,
        in_specs=[ANY] * 4,
        out_specs=[VMEM] * prompts,
        scratch_shapes=[pltpu.SemaphoreType.DMA((prompts, 4))],
        compiler_params=params(),
        name="pack",
    )(prompt_cache_keys, prompt_cache_values, span_raw_keys, span_raw_values)

    ring = [(i, (i + 1) % shards) for i in range(shards)]
    chunks = [[own[p]] for p in range(prompts)]
    for _ in range(shards - 1):
        for p in range(prompts):
            chunks[p].append(lax.ppermute(chunks[p][-1], "seq", ring))

    token = jnp.arange(ch * shards, dtype=jnp.int32)
    key_cos, key_sin = rotary_tables(span_offsets[:, None] + token[None, :])
    seq_index = lax.axis_index("seq")
    query_cos = lax.dynamic_slice_in_dim(key_cos, seq_index * ch, ch, 1)
    query_sin = lax.dynamic_slice_in_dim(key_sin, seq_index * ch, ch, 1)
    hot = row_request[:, None] == jnp.arange(prompts, dtype=jnp.int32)[None, :]
    row_begin = jnp.sum(jnp.where(hot, span_offsets[None, :], 0), axis=1)
    dec_positions = (row_begin + ch * shards + row_length)[:, None] + jnp.arange(
        steps, dtype=jnp.int32
    )[None, :]
    dec_cos, dec_sin = rotary_tables(dec_positions)

    queries = pl.pallas_call(
        functools.partial(query_kernel, used, per_kv),
        out_shape=jax.ShapeDtypeStruct((prompts, used, per_kv * ch, HEAD_WIDTH), bf16),
        grid=(prompts,),
        in_specs=[
            pl.BlockSpec((1, ch, q_width), lambda p: (p, 0, 0)),
            pl.BlockSpec((1, ch, HEAD_WIDTH), lambda p: (p, 0, 0)),
            pl.BlockSpec((1, ch, HEAD_WIDTH), lambda p: (p, 0, 0)),
        ],
        out_specs=pl.BlockSpec((1, used, per_kv * ch, HEAD_WIDTH), lambda p: (p, 0, 0, 0)),
        compiler_params=params(),
        name="queries",
    )(span_q, query_cos, query_sin)

    rows_step = math.gcd(rows_local, 4)
    dec_rows = rows_local * step_rows

    def own_lanes(i):
        return (i, 0, first_head(q_heads, kv_local) // used)

    def state_spec():
        return pl.BlockSpec((used, rows_step * step_rows, HEAD_WIDTH), lambda i: (0, i, 0))

    def state_shape(dtype):
        return jax.ShapeDtypeStruct((used, dec_rows, HEAD_WIDTH), dtype)

    state = pl.pallas_call(
        functools.partial(decode_kernel, used, per_kv, rows_step),
        out_shape=[state_shape(bf16), state_shape(f32), state_shape(f32), state_shape(f32)],
        grid=(rows_local // rows_step,),
        in_specs=[
            SMEM,
            pl.BlockSpec((rows_step, steps, q_width), lambda i: (i, 0, 0)),
            pl.BlockSpec((rows_step, steps, HEAD_WIDTH), lambda i: (i, 0, 0)),
            pl.BlockSpec((rows_step, steps, HEAD_WIDTH), lambda i: (i, 0, 0)),
            pl.BlockSpec((rows_step, gen, width), own_lanes),
            pl.BlockSpec((rows_step, gen, width), own_lanes),
            pl.BlockSpec((rows_step, steps, width), own_lanes),
            pl.BlockSpec((rows_step, steps, width), own_lanes),
        ],
        out_specs=[state_spec()] * 4,
        scratch_shapes=[
            pltpu.VMEM((rows_step, used, step_rows, HEAD_WIDTH), f32),
            pltpu.VMEM((rows_step, used, 16, HEAD_WIDTH), f32),
            pltpu.VMEM((rows_step, used, 16, HEAD_WIDTH), f32),
        ],
        compiler_params=params(),
        name="generated",
    )(
        row_length,
        decode_new_queries,
        dec_cos,
        dec_sin,
        generated_keys,
        generated_values,
        decode_new_keys,
        decode_new_values,
    )

    outs = ()
    keys_all = (pre + ch) * shards
    for p in range(prompts):
        ins = (span_offsets, row_request, *chunks[p], key_cos, key_sin, queries, *state)
        outs = pl.pallas_call(
            functools.partial(stage_kernel, p, used, per_kv, steps),
            out_shape=[
                jax.ShapeDtypeStruct(span_q.shape, bf16),
                jax.ShapeDtypeStruct(decode_new_queries.shape, bf16),
            ],
            grid=(1,),
            in_specs=[SMEM, SMEM]
            + [pl.BlockSpec((2, pre + ch, width), lambda i: (0, 0, 0))] * shards
            + [pl.BlockSpec((1, ch * shards, HEAD_WIDTH), lambda i, p=p: (p, 0, 0))] * 2
            + [pl.BlockSpec((1, used, per_kv * ch, HEAD_WIDTH), lambda i, p=p: (p, 0, 0, 0))]
            + [pl.BlockSpec((used, dec_rows, HEAD_WIDTH), lambda i: (0, 0, 0))] * 4
            + [ANY] * len(outs),
            out_specs=[pl.BlockSpec((1, ch, q_width), lambda i, p=p: (p, 0, 0)), ANY],
            scratch_shapes=[
                pltpu.VMEM((keys_all, width), bf16),
                pltpu.VMEM((keys_all, width), bf16),
                pltpu.VMEM((rows_local, steps, q_width), bf16),
                pltpu.SemaphoreType.DMA((rows_local,)),
            ],
            input_output_aliases={len(ins): 0, len(ins) + 1: 1} if outs else {},
            compiler_params=params(),
            name=f"stage_{p}",
        )(*ins, *outs)
    return tuple(outs)


def solution(mesh):
    in_specs = (
        P("group", "seq", ("head", "rep")),
        P("group", "seq", "head"),
        P("group", "seq", "head"),
        P("group", "seq", "head"),
        P("group", "seq", "head"),
        P("group"),
        P(("group", "seq"), None, ("head", "rep")),
        P(("group", "seq"), None, "head"),
        P(("group", "seq"), None, "head"),
        P(("group", "seq"), None, "head"),
        P(("group", "seq"), None, "head"),
        P(("group", "seq")),
        P(("group", "seq")),
    )
    out_specs = (P("group", "seq", ("head", "rep")), P(("group", "seq"), None, ("head", "rep")))
    return jax.shard_map(body, mesh=mesh, in_specs=in_specs, out_specs=out_specs, check_vma=False)
```

```python
import functools
import math

import jax
import jax.numpy as jnp
from jax import lax
from jax.experimental import pallas as pl
from jax.experimental.pallas import tpu as pltpu
from jax.sharding import PartitionSpec as P

QUERY_HEADS = 64
KEY_VALUE_HEADS = 8
HEAD_WIDTH = 128
HALF = HEAD_WIDTH // 2
GROUPS = QUERY_HEADS // KEY_VALUE_HEADS

very_low = -1e30
RATE = HEAD_WIDTH ** (-0.5) * math.log2(math.e)
HBM = pl.BlockSpec(memory_space=pltpu.HBM)
SMEM = pl.BlockSpec(memory_space=pltpu.SMEM)
VMEM = pl.BlockSpec(memory_space=pltpu.VMEM)
bf16 = jnp.bfloat16
f32 = jnp.float32


def tile(n):
    return pl.ds(n * HEAD_WIDTH, HEAD_WIDTH)


def iota(shape, axis):
    return lax.broadcasted_iota(jnp.int32, shape, axis)


def angle_tables(positions):
    lane = iota(positions.shape, 1)
    freqs = jnp.exp((lane % HALF).astype(f32) * (-2.0 * math.log(500000.0) / HEAD_WIDTH))
    angles = positions.astype(f32) * freqs
    return jnp.cos(angles), jnp.sin(angles)


def signed(sine):
    return jnp.where(iota(sine.shape, 1) < HALF, -sine, sine)


def rotate(x, cosine, sine):
    return x * cosine + pltpu.roll(x, HALF, axis=1) * sine


def token_tables(table, ch, row):
    cos_t, sin_t = table[0, pl.ds(0, ch), :], table[1, pl.ds(0, ch), :]
    cos_b, sin_b = table[0, pl.ds(row, 1), :], table[1, pl.ds(row, 1), :]
    return cos_b * cos_t - sin_b * sin_t, signed(sin_b * cos_t + cos_b * sin_t)


def first_head(q_heads, kv_local):
    block = lax.axis_index("head") * lax.axis_size("rep") + lax.axis_index("rep")
    return block * q_heads // GROUPS - lax.axis_index("head") * kv_local


def dot_nt(a, b):
    return lax.dot_general(a, b, (((1,), (1,)), ((), ())), preferred_element_type=f32)


def dot_tn(a, b):
    return lax.dot_general(a, b, (((0,), (0,)), ((), ())), preferred_element_type=f32)


def by_row(ref, lanes, step_rows, lookup=None):
    row = iota((1, lanes), 1) // step_rows
    out = jnp.zeros((1, lanes), jnp.int32)
    for r in range(lanes // step_rows):
        value = ref[r] if lookup is None else lookup[ref[r]]
        out = jnp.where(row == r, value, out)
    return out


def pack_keys_kernel(q_heads, kv_local, used, cache_ref, span_ref, out_ref, sem):
    prompts, pre, _ = cache_ref.shape
    ch = span_ref.shape[1]
    first = first_head(q_heads, kv_local)
    copies = []
    for p in range(prompts):
        for h in range(used):
            lanes = pl.ds(pl.multiple_of((first + h) * HEAD_WIDTH, HEAD_WIDTH), HEAD_WIDTH)
            for j, ref, rows in ((0, cache_ref, pl.ds(0, pre)), (1, span_ref, pl.ds(pre, ch))):
                copies.append(
                    pltpu.make_async_copy(
                        ref.at[p, :, lanes],
                        out_ref.at[rows, tile(h * prompts + p)],
                        sem.at[p, h, j],
                    )
                )
    for copy in copies:
        copy.start()
    for copy in copies:
        copy.wait()


def pack_values_kernel(q_heads, kv_local, used, cache_ref, span_ref, out_ref, sem):
    prompts, pre, _ = cache_ref.shape
    ch = span_ref.shape[1]
    first = first_head(q_heads, kv_local)
    lanes = pl.ds(pl.multiple_of(first * HEAD_WIDTH, HEAD_WIDTH), used * HEAD_WIDTH)
    copies = []
    for p in range(prompts):
        for j, ref, start, size in ((0, cache_ref, 0, pre), (1, span_ref, pre, ch)):
            copies.append(
                pltpu.make_async_copy(
                    ref.at[p, :, lanes],
                    out_ref.at[pl.ds(p * (pre + ch) + start, size), :],
                    sem.at[p, j],
                )
            )
    for copy in copies:
        copy.start()
    for copy in copies:
        copy.wait()


def prepare_kernel(
    shards,
    q_heads,
    kv_local,
    used,
    per_kv,
    begin_ref,
    request_ref,
    length_ref,
    span_q_ref,
    dec_q_ref,
    new_k_ref,
    new_v_ref,
    gen_k_ref,
    gen_v_ref,
    table_ref,
    q_ref,
    q_cat_ref,
    acc_ref,
    stat_ref,
    gk_scr,
    gv_scr,
    q_scr,
    n_scr,
    sem,
):
    prompts, ch, _ = span_q_ref.shape
    rows_local, steps, _ = dec_q_ref.shape
    gen = gen_k_ref.shape[1]
    step_rows = per_kv * steps
    dec_rows = rows_local * step_rows
    first = first_head(q_heads, kv_local)
    lanes = pl.ds(pl.multiple_of(first * HEAD_WIDTH, HEAD_WIDTH), used * HEAD_WIDTH)
    copies = [
        pltpu.make_async_copy(src.at[:, :, lanes], dst, sem.at[i])
        for i, (src, dst) in enumerate(((gen_k_ref, gk_scr), (gen_v_ref, gv_scr)))
    ]
    for copy in copies:
        copy.start()

    me = lax.axis_index("seq")
    base_rows = prompts * shards
    count = table_ref.shape[1]
    position = iota((count, HEAD_WIDTH), 0)
    for p in range(prompts):
        start = ch + p * shards
        row = iota((count, HEAD_WIDTH), 0)
        here = (row >= start) & (row < start + shards)
        position = jnp.where(here, begin_ref[p] + (row - start) * ch, position)
    for r in range(rows_local):
        start = ch + base_rows + r * steps
        row = iota((count, HEAD_WIDTH), 0)
        here = (row >= start) & (row < start + steps)
        length = begin_ref[request_ref[r]] + ch * shards + length_ref[r]
        position = jnp.where(here, length + row - start, position)
    cosine, sine = angle_tables(position)
    table_ref[0] = cosine
    table_ref[1] = sine

    for p in range(prompts):
        cosine, sine = token_tables(table_ref, ch, ch + p * shards + me)
        for h in range(used):
            for g in range(per_kv):
                x = span_q_ref[p, :, tile(h * per_kv + g)].astype(f32)
                q_ref[p, h, pl.ds(g * ch, ch), :] = rotate(x, cosine, sine).astype(bf16)

    n_scr[...] = jnp.zeros_like(n_scr)
    pad = n_scr.shape[2]
    for r in range(rows_local):
        rows = pl.ds(ch + base_rows + r * steps, steps)
        cosine = table_ref[0, rows, :]
        sine = signed(table_ref[1, rows, :])
        for h in range(used):
            for g in range(per_kv):
                x = dec_q_ref[r, :, tile(h * per_kv + g)].astype(f32)
                q_scr[h, pl.ds(r * step_rows + g * steps, steps), :] = rotate(x, cosine, sine)
            own = pl.ds(pl.multiple_of((first + h) * HEAD_WIDTH, HEAD_WIDTH), HEAD_WIDTH)
            n_scr[0, r * used + h, pl.ds(0, steps), :] = rotate(
                new_k_ref[r, :, own].astype(f32), cosine, sine
            )
            n_scr[1, r * used + h, pl.ds(0, steps), :] = new_v_ref[r, :, own].astype(f32)

    for h in range(used):
        for r in range(rows_local):
            rows = pl.ds(r * step_rows, step_rows)
            x = q_scr[h, rows, :]
            for p in range(prompts):
                q_cat_ref[h, rows, tile(p)] = jnp.where(request_ref[r] == p, x, 0.0).astype(bf16)

    for copy in copies:
        copy.wait()
    span = min(HEAD_WIDTH, dec_rows)
    group = span // step_rows
    lengths = by_row(length_ref, dec_rows, step_rows)
    begins = by_row(request_ref, dec_rows, step_rows, begin_ref)
    requests = by_row(request_ref, dec_rows, step_rows)
    key = iota((gen + pad, span), 0)
    lane = iota((gen + pad, span), 1)
    new_seen = (key >= gen) & (key - gen <= lane % steps)
    for h in range(used):
        stat_ref[h, pl.ds(2, 1), :] = begins.astype(f32)
        stat_ref[h, pl.ds(3, 1), :] = requests.astype(f32)
        for i in range(dec_rows // span):
            cols = pl.ds(i * span, span)
            q = q_scr[h, cols, :].astype(bf16)
            row = iota((span, HEAD_WIDTH), 0) // step_rows
            scores = None
            for j in range(group):
                r = i * group + j
                keys = jnp.concatenate(
                    [gk_scr[r, :, tile(h)], n_scr[0, r * used + h].astype(bf16)], axis=0
                )
                part = dot_nt(keys, jnp.where(row == j, q, jnp.zeros_like(q)))
                scores = part if scores is None else scores + part
            seen = (key < lengths[:, i * span : (i + 1) * span]) | new_seen
            scores = jnp.where(seen, scores, very_low)
            top = jnp.max(scores, axis=0, keepdims=True)
            weights = jnp.exp2((scores - top) * RATE)
            total = jnp.sum(weights, axis=0, keepdims=True)
            acc = None
            for j in range(group):
                r = i * group + j
                values = jnp.concatenate(
                    [gv_scr[r, :, tile(h)], n_scr[1, r * used + h].astype(bf16)], axis=0
                )
                part = dot_tn(
                    values, jnp.where(lane // step_rows == j, weights, 0.0).astype(bf16)
                )
                acc = part if acc is None else acc + part
            acc_ref[h, :, cols] = acc
            stat_ref[h, pl.ds(0, 1), cols] = top
            stat_ref[h, pl.ds(1, 1), cols] = total


def rotate_keys(chunk_ref, k_scr, table_ref, shards, prompts, used, pre, ch, shard, at):
    k_scr[pl.ds(at, pre), :] = chunk_ref[pl.ds(0, pre), :]
    for p in range(prompts):
        cosine, sine = token_tables(table_ref, ch, ch + p * shards + shard)
        for h in range(used):
            lanes = tile(h * prompts + p)
            x = chunk_ref[pl.ds(pre, ch), lanes].astype(f32)
            k_scr[pl.ds(at + pre, ch), lanes] = rotate(x, cosine, sine).astype(bf16)


def hide(scores, pre, begin, last):
    n, lanes = scores.shape
    low = scores[:pre]
    low = jnp.where(iota(low.shape, 0) < begin, low, very_low)
    high = scores[pre:]
    if last is not None:
        high = jnp.where(iota(high.shape, 0) <= last, high, very_low)
    return jnp.concatenate([low, high], axis=0)


def masked_stack(weights, requests, prompts):
    return jnp.concatenate(
        [jnp.where(requests == p, weights, 0.0).astype(bf16) for p in range(prompts)], axis=0
    )


def near_kernel(shards, used, ch, count, *refs):
    begin_ref = refs[0]
    keys, values = refs[1 : 1 + count], refs[1 + count : 1 + 2 * count]
    table_ref, q_ref, q_cat_ref, acc_in_ref, stat_in_ref = refs[1 + 2 * count : 6 + 2 * count]
    acc_ref, stat_ref, dec_acc_ref, dec_stat_ref, k_scr = refs[6 + 2 * count :]
    prompts, _, rows, _ = q_ref.shape
    size = keys[0].shape[0]
    dec_rows = q_cat_ref.shape[1]
    me = lax.axis_index("seq")
    pre = size - ch
    shard = [lax.rem(me + shards - c, shards) for c in range(count)]
    for c in range(count):
        rotate_keys(
            keys[c], k_scr, table_ref, shards, prompts, used, pre, ch, shard[c], c * size
        )
    token = me * ch + iota((1, rows), 1) % ch
    for h in range(used):
        requests = stat_in_ref[h, pl.ds(3, 1), :]
        begins = stat_in_ref[h, pl.ds(2, 1), :].astype(jnp.int32)
        for p in range(prompts):
            pieces = []
            for c in range(count):
                k = k_scr[pl.ds(c * size, size), tile(h * prompts + p)]
                pieces.append(
                    hide(
                        dot_nt(k, q_ref[p, h]),
                        pre,
                        begin_ref[p] - shard[c] * pre,
                        token - shard[c] * ch,
                    )
                )
            scores = jnp.concatenate(pieces, axis=0)
            top = jnp.max(scores, axis=0, keepdims=True)
            weights = jnp.exp2((scores - top) * RATE)
            total = jnp.sum(weights, axis=0, keepdims=True)
            v = jnp.concatenate(
                [ref[pl.ds(p * size, size), tile(h)] for ref in values], axis=0
            )
            acc_ref[p, h] = dot_tn(v, weights.astype(bf16))
            stat_ref[p, h, pl.ds(0, 1), :] = top
            stat_ref[p, h, pl.ds(1, 1), :] = total

        pieces = []
        for c in range(count):
            k = k_scr[pl.ds(c * size, size), pl.ds(h * prompts * HEAD_WIDTH, prompts * HEAD_WIDTH)]
            pieces.append(hide(dot_nt(k, q_cat_ref[h]), pre, begins - shard[c] * pre, None))
        scores = jnp.concatenate(pieces, axis=0)
        old_top = stat_in_ref[h, pl.ds(0, 1), :]
        top = jnp.maximum(jnp.max(scores, axis=0, keepdims=True), old_top)
        factor = jnp.exp2((old_top - top) * RATE)
        weights = jnp.exp2((scores - top) * RATE)
        total = jnp.sum(weights, axis=0, keepdims=True) + stat_in_ref[h, pl.ds(1, 1), :] * factor
        acc = acc_in_ref[h] * factor
        for c in range(count):
            w = masked_stack(weights[c * size : (c + 1) * size], requests, prompts)
            acc = acc + dot_tn(values[c][:, tile(h)], w)
        dec_acc_ref[h] = acc
        dec_stat_ref[h, pl.ds(0, 1), :] = top
        dec_stat_ref[h, pl.ds(1, 1), :] = total
        dec_stat_ref[h, pl.ds(2, 2), :] = stat_in_ref[h, pl.ds(2, 2), :]


def far_kernel(
    shards,
    used,
    ch,
    begin_ref,
    key_ref,
    table_ref,
    q_ref,
    q_cat_ref,
    acc_ref,
    stat_ref,
    dec_acc_ref,
    dec_stat_ref,
    base_ref,
    weight_ref,
    dec_base_ref,
    dec_weight_ref,
    k_scr,
):
    prompts, _, rows, _ = q_ref.shape
    size = key_ref.shape[0]
    me = lax.axis_index("seq")
    pre = size - ch
    shard = lax.rem(me + 1, shards)
    rotate_keys(key_ref, k_scr, table_ref, shards, prompts, used, pre, ch, shard, 0)
    token = me * ch + iota((1, rows), 1) % ch

    def finish(scores, old_top, old_total, old_acc):
        top = jnp.maximum(jnp.max(scores, axis=0, keepdims=True), old_top)
        factor = jnp.exp2((old_top - top) * RATE)
        weights = jnp.exp2((scores - top) * RATE)
        total = jnp.sum(weights, axis=0, keepdims=True) + old_total * factor
        inverse = 1.0 / total
        return weights * inverse, old_acc * (factor * inverse)

    for h in range(used):
        for p in range(prompts):
            scores = hide(
                dot_nt(k_scr[:, tile(h * prompts + p)], q_ref[p, h]),
                pre,
                begin_ref[p] - shard * pre,
                token - shard * ch,
            )
            weights, base = finish(
                scores, stat_ref[p, h, pl.ds(0, 1), :], stat_ref[p, h, pl.ds(1, 1), :], acc_ref[p, h]
            )
            weight_ref[p, h] = weights.T.astype(bf16)
            base_ref[p, h] = base.T
        begins = dec_stat_ref[h, pl.ds(2, 1), :].astype(jnp.int32)
        requests = dec_stat_ref[h, pl.ds(3, 1), :]
        k = k_scr[:, pl.ds(h * prompts * HEAD_WIDTH, prompts * HEAD_WIDTH)]
        scores = hide(dot_nt(k, q_cat_ref[h]), pre, begins - shard * pre, None)
        weights, base = finish(
            scores, dec_stat_ref[h, pl.ds(0, 1), :], dec_stat_ref[h, pl.ds(1, 1), :], dec_acc_ref[h]
        )
        stack = jnp.concatenate(
            [jnp.where(requests == p, weights, 0.0) for p in range(prompts)], axis=0
        )
        dec_weight_ref[h] = stack.T.astype(bf16)
        dec_base_ref[h] = base.T


def last_kernel(
    used,
    per_kv,
    steps,
    value_ref,
    base_ref,
    weight_ref,
    dec_base_ref,
    dec_weight_ref,
    span_ref,
    dec_ref,
    span_scr,
    dec_scr,
    sem,
):
    prompts, _, rows, size = weight_ref.shape
    ch = rows // per_kv
    step_rows = per_kv * steps
    copies = []
    for p in range(prompts):
        for h in range(used):
            out = base_ref[p, h] + jnp.dot(
                weight_ref[p, h],
                value_ref[pl.ds(p * size, size), tile(h)],
                preferred_element_type=f32,
            )
            out = out.astype(bf16)
            for g in range(per_kv):
                span_scr[p, :, tile(h * per_kv + g)] = out[g * ch : (g + 1) * ch]
        copies.append(pltpu.make_async_copy(span_scr.at[p], span_ref.at[p], sem.at[p]))
        copies[-1].start()
    for h in range(used):
        out = dec_base_ref[h] + jnp.dot(
            dec_weight_ref[h], value_ref[:, tile(h)], preferred_element_type=f32
        )
        for r in range(dec_scr.shape[0]):
            for g in range(per_kv):
                start = r * step_rows + g * steps
                dec_scr[r, :, tile(h * per_kv + g)] = out[start : start + steps].astype(bf16)
    copies.append(pltpu.make_async_copy(dec_scr, dec_ref, sem.at[prompts]))
    copies[-1].start()
    for copy in copies:
        copy.wait()


def body(
    span_q,
    span_raw_keys,
    span_raw_values,
    prompt_cache_keys,
    prompt_cache_values,
    span_offsets,
    decode_new_queries,
    decode_new_keys,
    decode_new_values,
    generated_keys,
    generated_values,
    row_request,
    row_length,
):
    prompts, ch, q_width = span_q.shape
    pre = prompt_cache_keys.shape[1]
    q_heads = q_width // HEAD_WIDTH
    kv_local = span_raw_keys.shape[2] // HEAD_WIDTH
    used = max(1, q_heads // GROUPS)
    per_kv = q_heads // used
    width = used * HEAD_WIDTH
    shards = lax.axis_size("seq")
    rows_local, steps = decode_new_queries.shape[:2]
    gen = generated_keys.shape[1]
    step_rows = per_kv * steps
    dec_rows = rows_local * step_rows
    rows = per_kv * ch
    size = pre + ch
    params = functools.partial(pltpu.CompilerParams, vmem_limit_bytes=16 << 20)
    shape = jax.ShapeDtypeStruct

    own_keys = pl.pallas_call(
        functools.partial(pack_keys_kernel, q_heads, kv_local, used),
        out_shape=shape((size, prompts * width), bf16),
        in_specs=[HBM, HBM],
        out_specs=VMEM,
        scratch_shapes=[pltpu.SemaphoreType.DMA((prompts, used, 2))],
        compiler_params=params(),
        name="pack_keys",
    )(prompt_cache_keys, span_raw_keys)
    own_values = pl.pallas_call(
        functools.partial(pack_values_kernel, q_heads, kv_local, used),
        out_shape=shape((prompts * size, width), bf16),
        in_specs=[HBM, HBM],
        out_specs=VMEM,
        scratch_shapes=[pltpu.SemaphoreType.DMA((prompts, 2))],
        compiler_params=params(),
        name="pack_values",
    )(prompt_cache_values, span_raw_values)

    ring = [(i, (i + 1) % shards) for i in range(shards)]
    keys = [own_keys]
    values = [own_values]
    for _ in range(shards - 1):
        keys.append(lax.ppermute(keys[-1], "seq", ring))
        values.append(lax.ppermute(values[-1], "seq", ring))

    table_rows = -(-(ch + prompts * shards + rows_local * steps) // 8) * 8
    table, queries, dec_queries, gen_acc, gen_stat = pl.pallas_call(
        functools.partial(prepare_kernel, shards, q_heads, kv_local, used, per_kv),
        out_shape=[
            shape((2, table_rows, HEAD_WIDTH), f32),
            shape((prompts, used, rows, HEAD_WIDTH), bf16),
            shape((used, dec_rows, prompts * HEAD_WIDTH), bf16),
            shape((used, HEAD_WIDTH, dec_rows), f32),
            shape((used, 8, dec_rows), f32),
        ],
        in_specs=[SMEM] * 3 + [VMEM] * 4 + [HBM] * 2,
        out_specs=[VMEM] * 5,
        scratch_shapes=[
            pltpu.VMEM((rows_local, gen, width), bf16),
            pltpu.VMEM((rows_local, gen, width), bf16),
            pltpu.VMEM((used, dec_rows, HEAD_WIDTH), f32),
            pltpu.VMEM((2, rows_local * used, 16, HEAD_WIDTH), f32),
            pltpu.SemaphoreType.DMA((2,)),
        ],
        compiler_params=params(),
        name="prepare",
    )(
        span_offsets,
        row_request,
        row_length,
        span_q,
        decode_new_queries,
        decode_new_keys,
        decode_new_values,
        generated_keys,
        generated_values,
    )

    count = shards - 1
    state = [
        shape((prompts, used, HEAD_WIDTH, rows), f32),
        shape((prompts, used, 8, rows), f32),
        shape((used, HEAD_WIDTH, dec_rows), f32),
        shape((used, 8, dec_rows), f32),
    ]
    near = pl.pallas_call(
        functools.partial(near_kernel, shards, used, ch, count),
        out_shape=state,
        in_specs=[SMEM] + [VMEM] * (2 * count + 5),
        out_specs=[VMEM] * 4,
        scratch_shapes=[pltpu.VMEM((count * size, prompts * width), bf16)],
        compiler_params=params(),
        name="near",
    )(span_offsets, *keys[:-1], *values[:-1], table, queries, dec_queries, gen_acc, gen_stat)

    far = pl.pallas_call(
        functools.partial(far_kernel, shards, used, ch),
        out_shape=[
            shape((prompts, used, rows, HEAD_WIDTH), f32),
            shape((prompts, used, rows, size), bf16),
            shape((used, dec_rows, HEAD_WIDTH), f32),
            shape((used, dec_rows, prompts * size), bf16),
        ],
        in_specs=[SMEM] + [VMEM] * 8,
        out_specs=[VMEM] * 4,
        scratch_shapes=[pltpu.VMEM((size, prompts * width), bf16)],
        compiler_params=params(),
        name="far",
    )(span_offsets, keys[-1], table, queries, dec_queries, *near)

    return tuple(
        pl.pallas_call(
            functools.partial(last_kernel, used, per_kv, steps),
            out_shape=[
                shape(span_q.shape, bf16),
                shape(decode_new_queries.shape, bf16),
            ],
            in_specs=[VMEM] * 5,
            out_specs=[HBM, HBM],
            scratch_shapes=[
                pltpu.VMEM(span_q.shape, bf16),
                pltpu.VMEM(decode_new_queries.shape, bf16),
                pltpu.SemaphoreType.DMA((prompts + 1,)),
            ],
            compiler_params=params(),
            name="last",
        )(values[-1], *far)
    )


def solution(mesh):
    in_specs = (
        P("group", "seq", ("head", "rep")),
        P("group", "seq", "head"),
        P("group", "seq", "head"),
        P("group", "seq", "head"),
        P("group", "seq", "head"),
        P("group"),
        P(("group", "seq"), None, ("head", "rep")),
        P(("group", "seq"), None, "head"),
        P(("group", "seq"), None, "head"),
        P(("group", "seq"), None, "head"),
        P(("group", "seq"), None, "head"),
        P(("group", "seq")),
        P(("group", "seq")),
    )
    out_specs = (P("group", "seq", ("head", "rep")), P(("group", "seq"), None, ("head", "rep")))
    return jax.shard_map(body, mesh=mesh, in_specs=in_specs, out_specs=out_specs, check_vma=False)
```

```python
import functools
import math

import jax
import jax.numpy as jnp
from jax import lax
from jax.experimental import pallas as pl
from jax.experimental.pallas import tpu as pltpu
from jax.sharding import PartitionSpec as P


QUERY_HEADS = 64
KEY_VALUE_HEADS = 8
HEAD_WIDTH = 128
HALF = HEAD_WIDTH // 2
GROUPS = QUERY_HEADS // KEY_VALUE_HEADS

very_low = -1e30
RATE = HEAD_WIDTH ** (-0.5) * math.log2(math.e)
ANY = pl.BlockSpec(memory_space=pl.ANY)
HBM = pl.BlockSpec(memory_space=pltpu.HBM)
SMEM = pl.BlockSpec(memory_space=pltpu.SMEM)
VMEM = pl.BlockSpec(memory_space=pltpu.VMEM)
bf16 = jnp.bfloat16
f32 = jnp.float32


def in_hbm(*arrays):
    return [pltpu.with_memory_space_constraint(array, pltpu.HBM) for array in arrays]


def cost(micros):
    return pl.CostEstimate(
        flops=int(micros * 1e9), bytes_accessed=int(micros * 3e6), transcendentals=0
    )


def tile(n):
    return pl.ds(n * HEAD_WIDTH, HEAD_WIDTH)


def iota(shape, axis):
    return lax.broadcasted_iota(jnp.int32, shape, axis)


def angle_tables(positions):
    lane = iota(positions.shape, 1)
    freqs = jnp.exp((lane % HALF).astype(f32) * (-2.0 * math.log(500000.0) / HEAD_WIDTH))
    angles = positions.astype(f32) * freqs
    return jnp.cos(angles), jnp.sin(angles)


def signed(sine):
    return jnp.where(iota(sine.shape, 1) < HALF, -sine, sine)


def rotate(x, cosine, sine):
    return x * cosine + pltpu.roll(x, HALF, axis=1) * sine


def token_tables(table, ch, row):
    cos_t, sin_t = table[0, pl.ds(0, ch), :], table[1, pl.ds(0, ch), :]
    cos_b, sin_b = table[0, pl.ds(row, 1), :], table[1, pl.ds(row, 1), :]
    return cos_b * cos_t - sin_b * sin_t, signed(sin_b * cos_t + cos_b * sin_t)


def first_head(q_heads, kv_local):
    block = lax.axis_index("head") * lax.axis_size("rep") + lax.axis_index("rep")
    return block * q_heads // GROUPS - lax.axis_index("head") * kv_local


def dot_nt(a, b):
    return lax.dot_general(a, b, (((1,), (1,)), ((), ())), preferred_element_type=f32)


def dot_tn(a, b):
    return lax.dot_general(a, b, (((0,), (0,)), ((), ())), preferred_element_type=f32)


def by_row(ref, lanes, step_rows, lookup=None):
    row = iota((1, lanes), 1) // step_rows
    out = jnp.zeros((1, lanes), jnp.int32)
    for r in range(lanes // step_rows):
        value = ref[r] if lookup is None else lookup[ref[r]]
        out = jnp.where(row == r, value, out)
    return out


def pack_keys_kernel(q_heads, kv_local, used, cache_ref, span_ref, out_ref, sem):
    prompts, pre, _ = cache_ref.shape
    ch = span_ref.shape[1]
    first = first_head(q_heads, kv_local)
    copies = []
    for p in range(prompts):
        for h in range(used):
            lanes = pl.ds(pl.multiple_of((first + h) * HEAD_WIDTH, HEAD_WIDTH), HEAD_WIDTH)
            for j, ref, rows in ((0, cache_ref, pl.ds(0, pre)), (1, span_ref, pl.ds(pre, ch))):
                copies.append(
                    pltpu.make_async_copy(
                        ref.at[p, :, lanes],
                        out_ref.at[rows, tile(h * prompts + p)],
                        sem.at[p, h, j],
                    )
                )
    for copy in copies:
        copy.start()
    for copy in copies:
        copy.wait()


def pack_values_kernel(q_heads, kv_local, used, cache_ref, span_ref, after_ref, out_ref, sem):
    del after_ref
    prompts, pre, _ = cache_ref.shape
    ch = span_ref.shape[1]
    first = first_head(q_heads, kv_local)
    lanes = pl.ds(pl.multiple_of(first * HEAD_WIDTH, HEAD_WIDTH), used * HEAD_WIDTH)
    copies = []
    for p in range(prompts):
        for j, ref, start, size in ((0, cache_ref, 0, pre), (1, span_ref, pre, ch)):
            copies.append(
                pltpu.make_async_copy(
                    ref.at[p, :, lanes],
                    out_ref.at[pl.ds(p * (pre + ch) + start, size), :],
                    sem.at[p, j],
                )
            )
    for copy in copies:
        copy.start()
    for copy in copies:
        copy.wait()


def prepare_kernel(
    shards,
    q_heads,
    kv_local,
    used,
    per_kv,
    begin_ref,
    request_ref,
    length_ref,
    span_q_ref,
    dec_q_ref,
    new_k_ref,
    new_v_ref,
    gen_k_ref,
    gen_v_ref,
    table_ref,
    q_ref,
    q_cat_ref,
    acc_ref,
    stat_ref,
    sq_scr,
    dq_scr,
    nk_scr,
    nv_scr,
    gk_scr,
    gv_scr,
    q_scr,
    n_scr,
    sem,
):
    prompts, ch, _ = span_q_ref.shape
    rows_local, steps, _ = dec_q_ref.shape
    gen = gen_k_ref.shape[1]
    step_rows = per_kv * steps
    dec_rows = rows_local * step_rows
    first = first_head(q_heads, kv_local)
    lanes = pl.ds(pl.multiple_of(first * HEAD_WIDTH, HEAD_WIDTH), used * HEAD_WIDTH)
    copies = [
        pltpu.make_async_copy(span_q_ref, sq_scr, sem.at[0]),
        pltpu.make_async_copy(dec_q_ref, dq_scr, sem.at[1]),
        pltpu.make_async_copy(new_k_ref.at[:, :, lanes], nk_scr, sem.at[2]),
        pltpu.make_async_copy(new_v_ref.at[:, :, lanes], nv_scr, sem.at[3]),
        pltpu.make_async_copy(gen_k_ref.at[:, :, lanes], gk_scr, sem.at[4]),
        pltpu.make_async_copy(gen_v_ref.at[:, :, lanes], gv_scr, sem.at[5]),
    ]
    for copy in copies:
        copy.start()

    me = lax.axis_index("seq")
    base_rows = prompts * shards
    count = table_ref.shape[1]
    position = iota((count, HEAD_WIDTH), 0)
    for p in range(prompts):
        start = ch + p * shards
        row = iota((count, HEAD_WIDTH), 0)
        here = (row >= start) & (row < start + shards)
        position = jnp.where(here, begin_ref[p] + (row - start) * ch, position)
    for r in range(rows_local):
        start = ch + base_rows + r * steps
        row = iota((count, HEAD_WIDTH), 0)
        here = (row >= start) & (row < start + steps)
        length = begin_ref[request_ref[r]] + ch * shards + length_ref[r]
        position = jnp.where(here, length + row - start, position)
    cosine, sine = angle_tables(position)
    table_ref[0] = cosine
    table_ref[1] = sine

    copies[0].wait()
    for p in range(prompts):
        cosine, sine = token_tables(table_ref, ch, ch + p * shards + me)
        for h in range(used):
            for g in range(per_kv):
                x = sq_scr[p, :, tile(h * per_kv + g)].astype(f32)
                q_ref[p, h, pl.ds(g * ch, ch), :] = rotate(x, cosine, sine).astype(bf16)

    for copy in copies[1:4]:
        copy.wait()
    n_scr[...] = jnp.zeros_like(n_scr)
    pad = n_scr.shape[2]
    for r in range(rows_local):
        rows = pl.ds(ch + base_rows + r * steps, steps)
        cosine = table_ref[0, rows, :]
        sine = signed(table_ref[1, rows, :])
        for h in range(used):
            for g in range(per_kv):
                x = dq_scr[r, :, tile(h * per_kv + g)].astype(f32)
                q_scr[h, pl.ds(r * step_rows + g * steps, steps), :] = rotate(x, cosine, sine)
            n_scr[0, r * used + h, pl.ds(0, steps), :] = rotate(
                nk_scr[r, :, tile(h)].astype(f32), cosine, sine
            )
            n_scr[1, r * used + h, pl.ds(0, steps), :] = nv_scr[r, :, tile(h)].astype(f32)

    for h in range(used):
        for r in range(rows_local):
            rows = pl.ds(r * step_rows, step_rows)
            x = q_scr[h, rows, :]
            for p in range(prompts):
                q_cat_ref[h, rows, tile(p)] = jnp.where(request_ref[r] == p, x, 0.0).astype(bf16)

    for copy in copies[4:]:
        copy.wait()
    span = min(HEAD_WIDTH, dec_rows)
    group = span // step_rows
    lengths = by_row(length_ref, dec_rows, step_rows)
    begins = by_row(request_ref, dec_rows, step_rows, begin_ref)
    requests = by_row(request_ref, dec_rows, step_rows)
    key = iota((gen + pad, span), 0)
    lane = iota((gen + pad, span), 1)
    new_seen = (key >= gen) & (key - gen <= lane % steps)
    for h in range(used):
        stat_ref[h, pl.ds(2, 1), :] = begins.astype(f32)
        stat_ref[h, pl.ds(3, 1), :] = requests.astype(f32)
        for i in range(dec_rows // span):
            cols = pl.ds(i * span, span)
            q = q_scr[h, cols, :].astype(bf16)
            row = iota((span, HEAD_WIDTH), 0) // step_rows
            scores = None
            for j in range(group):
                r = i * group + j
                keys = jnp.concatenate(
                    [gk_scr[r, :, tile(h)], n_scr[0, r * used + h].astype(bf16)], axis=0
                )
                part = dot_nt(keys, jnp.where(row == j, q, jnp.zeros_like(q)))
                scores = part if scores is None else scores + part
            seen = (key < lengths[:, i * span : (i + 1) * span]) | new_seen
            scores = jnp.where(seen, scores, very_low)
            top = jnp.max(scores, axis=0, keepdims=True)
            weights = jnp.exp2((scores - top) * RATE)
            total = jnp.sum(weights, axis=0, keepdims=True)
            acc = None
            for j in range(group):
                r = i * group + j
                values = jnp.concatenate(
                    [gv_scr[r, :, tile(h)], n_scr[1, r * used + h].astype(bf16)], axis=0
                )
                part = dot_tn(
                    values, jnp.where(lane // step_rows == j, weights, 0.0).astype(bf16)
                )
                acc = part if acc is None else acc + part
            acc_ref[h, :, cols] = acc
            stat_ref[h, pl.ds(0, 1), cols] = top
            stat_ref[h, pl.ds(1, 1), cols] = total


def rotate_keys(chunk_ref, k_scr, table_ref, shards, prompts, used, pre, ch, shard, at):
    k_scr[pl.ds(at, pre), :] = chunk_ref[pl.ds(0, pre), :]
    for p in range(prompts):
        cosine, sine = token_tables(table_ref, ch, ch + p * shards + shard)
        for h in range(used):
            lanes = tile(h * prompts + p)
            x = chunk_ref[pl.ds(pre, ch), lanes].astype(f32)
            k_scr[pl.ds(at + pre, ch), lanes] = rotate(x, cosine, sine).astype(bf16)


def hide(scores, pre, begin, last):
    low = scores[:pre]
    low = jnp.where(iota(low.shape, 0) < begin, low, very_low)
    high = scores[pre:]
    if last is not None:
        high = jnp.where(iota(high.shape, 0) <= last, high, very_low)
    return jnp.concatenate([low, high], axis=0)


def masked_stack(weights, requests, prompts):
    return jnp.concatenate(
        [jnp.where(requests == p, weights, 0.0).astype(bf16) for p in range(prompts)], axis=0
    )


def near_kernel(shards, used, ch, hops, *refs):
    count = len(hops)
    begin_ref = refs[0]
    keys, values = refs[1 : 1 + count], refs[1 + count : 1 + 2 * count]
    table_ref, q_ref, q_cat_ref, acc_in_ref, stat_in_ref = refs[1 + 2 * count : 6 + 2 * count]
    before = refs[6 + 2 * count : -5]
    acc_ref, stat_ref, dec_acc_ref, dec_stat_ref, k_scr = refs[-5:]
    prompts, _, rows, _ = q_ref.shape
    size = keys[0].shape[0]
    me = lax.axis_index("seq")
    pre = size - ch
    shard = [lax.rem(me + shards - hop, shards) for hop in hops]
    for c in range(count):
        rotate_keys(
            keys[c], k_scr, table_ref, shards, prompts, used, pre, ch, shard[c], c * size
        )
    token = me * ch + iota((1, rows), 1) % ch
    for h in range(used):
        requests = stat_in_ref[h, pl.ds(3, 1), :]
        begins = stat_in_ref[h, pl.ds(2, 1), :].astype(jnp.int32)
        for p in range(prompts):
            pieces = []
            for c in range(count):
                k = k_scr[pl.ds(c * size, size), tile(h * prompts + p)]
                pieces.append(
                    hide(
                        dot_nt(k, q_ref[p, h]),
                        pre,
                        begin_ref[p] - shard[c] * pre,
                        token - shard[c] * ch,
                    )
                )
            scores = jnp.concatenate(pieces, axis=0)
            top = jnp.max(scores, axis=0, keepdims=True)
            if before:
                old_top = before[1][p, h, pl.ds(0, 1), :]
                top = jnp.maximum(top, old_top)
            weights = jnp.exp2((scores - top) * RATE)
            total = jnp.sum(weights, axis=0, keepdims=True)
            v = jnp.concatenate(
                [ref[pl.ds(p * size, size), tile(h)] for ref in values], axis=0
            )
            acc = dot_tn(v, weights.astype(bf16))
            if before:
                factor = jnp.exp2((old_top - top) * RATE)
                total = total + before[1][p, h, pl.ds(1, 1), :] * factor
                acc = acc + before[0][p, h] * factor
            acc_ref[p, h] = acc
            stat_ref[p, h, pl.ds(0, 1), :] = top
            stat_ref[p, h, pl.ds(1, 1), :] = total

        pieces = []
        for c in range(count):
            k = k_scr[pl.ds(c * size, size), pl.ds(h * prompts * HEAD_WIDTH, prompts * HEAD_WIDTH)]
            pieces.append(hide(dot_nt(k, q_cat_ref[h]), pre, begins - shard[c] * pre, None))
        scores = jnp.concatenate(pieces, axis=0)
        old_top = stat_in_ref[h, pl.ds(0, 1), :]
        top = jnp.maximum(jnp.max(scores, axis=0, keepdims=True), old_top)
        factor = jnp.exp2((old_top - top) * RATE)
        weights = jnp.exp2((scores - top) * RATE)
        total = jnp.sum(weights, axis=0, keepdims=True) + stat_in_ref[h, pl.ds(1, 1), :] * factor
        acc = acc_in_ref[h] * factor
        for c in range(count):
            w = masked_stack(weights[c * size : (c + 1) * size], requests, prompts)
            acc = acc + dot_tn(values[c][:, tile(h)], w)
        dec_acc_ref[h] = acc
        dec_stat_ref[h, pl.ds(0, 1), :] = top
        dec_stat_ref[h, pl.ds(1, 1), :] = total
        dec_stat_ref[h, pl.ds(2, 2), :] = stat_in_ref[h, pl.ds(2, 2), :]


def far_kernel(
    shards,
    used,
    ch,
    begin_ref,
    key_ref,
    table_ref,
    q_ref,
    q_cat_ref,
    acc_ref,
    stat_ref,
    dec_acc_ref,
    dec_stat_ref,
    base_ref,
    weight_ref,
    dec_base_ref,
    dec_weight_ref,
    k_scr,
):
    prompts, _, rows, _ = q_ref.shape
    size = key_ref.shape[0]
    me = lax.axis_index("seq")
    pre = size - ch
    shard = lax.rem(me + 1, shards)
    rotate_keys(key_ref, k_scr, table_ref, shards, prompts, used, pre, ch, shard, 0)
    token = me * ch + iota((1, rows), 1) % ch

    def finish(scores, old_top, old_total, old_acc):
        top = jnp.maximum(jnp.max(scores, axis=0, keepdims=True), old_top)
        factor = jnp.exp2((old_top - top) * RATE)
        weights = jnp.exp2((scores - top) * RATE)
        total = jnp.sum(weights, axis=0, keepdims=True) + old_total * factor
        inverse = 1.0 / total
        return weights * inverse, old_acc * (factor * inverse)

    for h in range(used):
        for p in range(prompts):
            scores = hide(
                dot_nt(k_scr[:, tile(h * prompts + p)], q_ref[p, h]),
                pre,
                begin_ref[p] - shard * pre,
                token - shard * ch,
            )
            weights, base = finish(
                scores, stat_ref[p, h, pl.ds(0, 1), :], stat_ref[p, h, pl.ds(1, 1), :], acc_ref[p, h]
            )
            weight_ref[p, h] = weights.T.astype(bf16)
            base_ref[p, h] = base.T
        begins = dec_stat_ref[h, pl.ds(2, 1), :].astype(jnp.int32)
        requests = dec_stat_ref[h, pl.ds(3, 1), :]
        k = k_scr[:, pl.ds(h * prompts * HEAD_WIDTH, prompts * HEAD_WIDTH)]
        scores = hide(dot_nt(k, q_cat_ref[h]), pre, begins - shard * pre, None)
        weights, base = finish(
            scores, dec_stat_ref[h, pl.ds(0, 1), :], dec_stat_ref[h, pl.ds(1, 1), :], dec_acc_ref[h]
        )
        stack = jnp.concatenate(
            [jnp.where(requests == p, weights, 0.0) for p in range(prompts)], axis=0
        )
        dec_weight_ref[h] = stack.T.astype(bf16)
        dec_base_ref[h] = base.T


def last_kernel(
    used,
    per_kv,
    steps,
    value_ref,
    base_ref,
    weight_ref,
    dec_base_ref,
    dec_weight_ref,
    span_ref,
    dec_ref,
    span_scr,
    dec_scr,
    sem,
):
    prompts, _, rows, size = weight_ref.shape
    ch = rows // per_kv
    step_rows = per_kv * steps
    copies = []
    for p in range(prompts):
        for h in range(used):
            out = base_ref[p, h] + jnp.dot(
                weight_ref[p, h],
                value_ref[pl.ds(p * size, size), tile(h)],
                preferred_element_type=f32,
            )
            out = out.astype(bf16)
            for g in range(per_kv):
                span_scr[p, :, tile(h * per_kv + g)] = out[g * ch : (g + 1) * ch]
        copies.append(pltpu.make_async_copy(span_scr.at[p], span_ref.at[p], sem.at[p]))
        copies[-1].start()
    for h in range(used):
        out = dec_base_ref[h] + jnp.dot(
            dec_weight_ref[h], value_ref[:, tile(h)], preferred_element_type=f32
        )
        for r in range(dec_scr.shape[0]):
            for g in range(per_kv):
                start = r * step_rows + g * steps
                dec_scr[r, :, tile(h * per_kv + g)] = out[start : start + steps].astype(bf16)
    copies.append(pltpu.make_async_copy(dec_scr, dec_ref, sem.at[prompts]))
    copies[-1].start()
    for copy in copies:
        copy.wait()


def body(
    span_q,
    span_raw_keys,
    span_raw_values,
    prompt_cache_keys,
    prompt_cache_values,
    span_offsets,
    decode_new_queries,
    decode_new_keys,
    decode_new_values,
    generated_keys,
    generated_values,
    row_request,
    row_length,
):
    prompts, ch, q_width = span_q.shape
    pre = prompt_cache_keys.shape[1]
    q_heads = q_width // HEAD_WIDTH
    kv_local = span_raw_keys.shape[2] // HEAD_WIDTH
    used = max(1, q_heads // GROUPS)
    per_kv = q_heads // used
    width = used * HEAD_WIDTH
    shards = lax.axis_size("seq")
    rows_local, steps = decode_new_queries.shape[:2]
    gen = generated_keys.shape[1]
    step_rows = per_kv * steps
    dec_rows = rows_local * step_rows
    rows = per_kv * ch
    size = pre + ch
    params = functools.partial(pltpu.CompilerParams, vmem_limit_bytes=16 << 20)
    shape = jax.ShapeDtypeStruct

    own_keys = pl.pallas_call(
        functools.partial(pack_keys_kernel, q_heads, kv_local, used),
        out_shape=shape((size, prompts * width), bf16),
        in_specs=[HBM, HBM],
        out_specs=VMEM,
        scratch_shapes=[pltpu.SemaphoreType.DMA((prompts, used, 2))],
        compiler_params=params(),
        cost_estimate=cost(1),
        name="pack_keys",
    )(*in_hbm(prompt_cache_keys, span_raw_keys))
    own_values = pl.pallas_call(
        functools.partial(pack_values_kernel, q_heads, kv_local, used),
        out_shape=shape((prompts * size, width), bf16),
        in_specs=[HBM, HBM, ANY],
        out_specs=VMEM,
        scratch_shapes=[pltpu.SemaphoreType.DMA((prompts, 2))],
        compiler_params=params(),
        cost_estimate=cost(1),
        name="pack_values",
    )(*in_hbm(prompt_cache_values, span_raw_values), own_keys)

    ring = [(i, (i + 1) % shards) for i in range(shards)]
    keys = [own_keys]
    values = [own_values]
    for _ in range(1, shards):
        keys.append(lax.ppermute(keys[-1], "seq", ring))
        values.append(lax.ppermute(values[-1], "seq", ring))

    table_rows = -(-(ch + prompts * shards + rows_local * steps) // 8) * 8
    table, queries, dec_queries, gen_acc, gen_stat = pl.pallas_call(
        functools.partial(prepare_kernel, shards, q_heads, kv_local, used, per_kv),
        out_shape=[
            shape((2, table_rows, HEAD_WIDTH), f32),
            shape((prompts, used, rows, HEAD_WIDTH), bf16),
            shape((used, dec_rows, prompts * HEAD_WIDTH), bf16),
            shape((used, HEAD_WIDTH, dec_rows), f32),
            shape((used, 8, dec_rows), f32),
        ],
        in_specs=[SMEM] * 3 + [HBM] * 6,
        out_specs=[VMEM] * 5,
        scratch_shapes=[
            pltpu.VMEM(span_q.shape, bf16),
            pltpu.VMEM(decode_new_queries.shape, bf16),
            pltpu.VMEM((rows_local, steps, width), bf16),
            pltpu.VMEM((rows_local, steps, width), bf16),
            pltpu.VMEM((rows_local, gen, width), bf16),
            pltpu.VMEM((rows_local, gen, width), bf16),
            pltpu.VMEM((used, dec_rows, HEAD_WIDTH), f32),
            pltpu.VMEM((2, rows_local * used, 16, HEAD_WIDTH), f32),
            pltpu.SemaphoreType.DMA((6,)),
        ],
        compiler_params=params(),
        cost_estimate=cost(3),
        name="prepare",
    )(
        span_offsets,
        row_request,
        row_length,
        *in_hbm(
            span_q,
            decode_new_queries,
            decode_new_keys,
            decode_new_values,
            generated_keys,
            generated_values,
        ),
    )

    prompt_state = [
        shape((prompts, used, HEAD_WIDTH, rows), f32),
        shape((prompts, used, 8, rows), f32),
    ]
    row_state = [shape((used, HEAD_WIDTH, dec_rows), f32), shape((used, 8, dec_rows), f32)]
    near = [gen_acc, gen_stat]
    for step in range(1, max(2, shards - 1)):
        hops = [hop for hop in ([0, 1] if step == 1 else [step]) if hop < shards - 1]
        ins = [span_offsets, *[keys[hop] for hop in hops], *[values[hop] for hop in hops]]
        ins += [table, queries, dec_queries, *near[-2:], *near[:-2]]
        near = pl.pallas_call(
            functools.partial(near_kernel, shards, used, ch, hops),
            out_shape=prompt_state + row_state,
            in_specs=[SMEM] + [VMEM] * (len(ins) - 1),
            out_specs=[VMEM] * 4,
            scratch_shapes=[pltpu.VMEM((len(hops) * size, prompts * width), bf16)],
            compiler_params=params(),
            cost_estimate=cost(3),
        )(*ins)

    far = pl.pallas_call(
        functools.partial(far_kernel, shards, used, ch),
        out_shape=[
            shape((prompts, used, rows, HEAD_WIDTH), f32),
            shape((prompts, used, rows, size), bf16),
            shape((used, dec_rows, HEAD_WIDTH), f32),
            shape((used, dec_rows, prompts * size), bf16),
        ],
        in_specs=[SMEM] + [VMEM] * 8,
        out_specs=[VMEM] * 4,
        scratch_shapes=[pltpu.VMEM((size, prompts * width), bf16)],
        compiler_params=params(),
        cost_estimate=cost(2),
        name="far",
    )(span_offsets, keys[-1], table, queries, dec_queries, *near)

    return tuple(
        pl.pallas_call(
            functools.partial(last_kernel, used, per_kv, steps),
            out_shape=[
                shape(span_q.shape, bf16),
                shape(decode_new_queries.shape, bf16),
            ],
            in_specs=[VMEM] * 5,
            out_specs=[HBM, HBM],
            scratch_shapes=[
                pltpu.VMEM(span_q.shape, bf16),
                pltpu.VMEM(decode_new_queries.shape, bf16),
                pltpu.SemaphoreType.DMA((prompts + 1,)),
            ],
            compiler_params=params(),
            cost_estimate=cost(1),
        name="last",
        )(values[-1], *far)
    )


def solution(mesh):
    in_specs = (
        P("group", "seq", ("head", "rep")),
        P("group", "seq", "head"),
        P("group", "seq", "head"),
        P("group", "seq", "head"),
        P("group", "seq", "head"),
        P("group"),
        P(("group", "seq"), None, ("head", "rep")),
        P(("group", "seq"), None, "head"),
        P(("group", "seq"), None, "head"),
        P(("group", "seq"), None, "head"),
        P(("group", "seq"), None, "head"),
        P(("group", "seq")),
        P(("group", "seq")),
    )
    out_specs = (P("group", "seq", ("head", "rep")), P(("group", "seq"), None, ("head", "rep")))
    return jax.shard_map(body, mesh=mesh, in_specs=in_specs, out_specs=out_specs, check_vma=False)
```

```python
import functools
import math

import jax
import jax.numpy as jnp
from jax import lax
from jax.experimental import pallas as pl
from jax.experimental.pallas import tpu as pltpu
from jax.sharding import PartitionSpec as P


QUERY_HEADS = 64
KEY_VALUE_HEADS = 8
HEAD_WIDTH = 128
HALF = HEAD_WIDTH // 2
GROUPS = QUERY_HEADS // KEY_VALUE_HEADS

very_low = -1e30
RATE = HEAD_WIDTH ** (-0.5) * math.log2(math.e)
ANY = pl.BlockSpec(memory_space=pl.ANY)
HBM = pl.BlockSpec(memory_space=pltpu.HBM)
SMEM = pl.BlockSpec(memory_space=pltpu.SMEM)
VMEM = pl.BlockSpec(memory_space=pltpu.VMEM)
bf16 = jnp.bfloat16
f32 = jnp.float32


def in_hbm(*arrays):
    return [pltpu.with_memory_space_constraint(array, pltpu.HBM) for array in arrays]


def cost(micros):
    return pl.CostEstimate(
        flops=int(micros * 1e9), bytes_accessed=int(micros * 3e6), transcendentals=0
    )


def tile(n):
    return pl.ds(n * HEAD_WIDTH, HEAD_WIDTH)


def iota(shape, axis):
    return lax.broadcasted_iota(jnp.int32, shape, axis)


def angle_tables(positions):
    lane = iota(positions.shape, 1)
    freqs = jnp.exp((lane % HALF).astype(f32) * (-2.0 * math.log(500000.0) / HEAD_WIDTH))
    angles = positions.astype(f32) * freqs
    return jnp.cos(angles), jnp.sin(angles)


def signed(sine):
    return jnp.where(iota(sine.shape, 1) < HALF, -sine, sine)


def rotate(x, cosine, sine):
    return x * cosine + pltpu.roll(x, HALF, axis=1) * sine


def token_tables(table, ch, row):
    cos_t, sin_t = table[0, pl.ds(0, ch), :], table[1, pl.ds(0, ch), :]
    cos_b, sin_b = table[0, pl.ds(row, 1), :], table[1, pl.ds(row, 1), :]
    return cos_b * cos_t - sin_b * sin_t, signed(sin_b * cos_t + cos_b * sin_t)


def first_head(q_heads, kv_local):
    block = lax.axis_index("head") * lax.axis_size("rep") + lax.axis_index("rep")
    return block * q_heads // GROUPS - lax.axis_index("head") * kv_local


def ring_order(shards):
    return [*range(0, shards, 2), *reversed(range(1, shards, 2))]


def ring_source(me, shards, hop):
    place = jnp.where(lax.rem(me, 2) == 0, me // 2, shards - 1 - me // 2)
    place = lax.rem(place + shards - hop, shards)
    return jnp.where(place < (shards + 1) // 2, 2 * place, 2 * (shards - 1 - place) + 1)


def dot_nt(a, b):
    return lax.dot_general(a, b, (((1,), (1,)), ((), ())), preferred_element_type=f32)


def dot_tn(a, b):
    return lax.dot_general(a, b, (((0,), (0,)), ((), ())), preferred_element_type=f32)


def by_row(ref, lanes, step_rows, lookup=None):
    row = iota((1, lanes), 1) // step_rows
    out = jnp.zeros((1, lanes), jnp.int32)
    for r in range(lanes // step_rows):
        value = ref[r] if lookup is None else lookup[ref[r]]
        out = jnp.where(row == r, value, out)
    return out


def pack_keys_kernel(q_heads, kv_local, used, cache_ref, span_ref, out_ref, sem):
    prompts, pre, _ = cache_ref.shape
    ch = span_ref.shape[1]
    first = first_head(q_heads, kv_local)
    copies = []
    for p in range(prompts):
        for h in range(used):
            lanes = pl.ds(pl.multiple_of((first + h) * HEAD_WIDTH, HEAD_WIDTH), HEAD_WIDTH)
            for j, ref, rows in ((0, cache_ref, pl.ds(0, pre)), (1, span_ref, pl.ds(pre, ch))):
                copies.append(
                    pltpu.make_async_copy(
                        ref.at[p, :, lanes],
                        out_ref.at[rows, tile(h * prompts + p)],
                        sem.at[p, h, j],
                    )
                )
    for copy in copies:
        copy.start()
    for copy in copies:
        copy.wait()


def pack_values_kernel(q_heads, kv_local, used, cache_ref, span_ref, after_ref, out_ref, sem):
    del after_ref
    prompts, pre, _ = cache_ref.shape
    ch = span_ref.shape[1]
    first = first_head(q_heads, kv_local)
    lanes = pl.ds(pl.multiple_of(first * HEAD_WIDTH, HEAD_WIDTH), used * HEAD_WIDTH)
    copies = []
    for p in range(prompts):
        for j, ref, start, size in ((0, cache_ref, 0, pre), (1, span_ref, pre, ch)):
            copies.append(
                pltpu.make_async_copy(
                    ref.at[p, :, lanes],
                    out_ref.at[pl.ds(p * (pre + ch) + start, size), :],
                    sem.at[p, j],
                )
            )
    for copy in copies:
        copy.start()
    for copy in copies:
        copy.wait()


def prepare_kernel(
    shards,
    q_heads,
    kv_local,
    used,
    per_kv,
    begin_ref,
    request_ref,
    length_ref,
    span_q_ref,
    dec_q_ref,
    new_k_ref,
    new_v_ref,
    gen_k_ref,
    gen_v_ref,
    table_ref,
    q_ref,
    q_cat_ref,
    acc_ref,
    stat_ref,
    sq_scr,
    dq_scr,
    nk_scr,
    nv_scr,
    gk_scr,
    gv_scr,
    q_scr,
    n_scr,
    sem,
):
    prompts, ch, _ = span_q_ref.shape
    rows_local, steps, _ = dec_q_ref.shape
    gen = gen_k_ref.shape[1]
    step_rows = per_kv * steps
    dec_rows = rows_local * step_rows
    first = first_head(q_heads, kv_local)
    lanes = pl.ds(pl.multiple_of(first * HEAD_WIDTH, HEAD_WIDTH), used * HEAD_WIDTH)
    copies = [
        pltpu.make_async_copy(span_q_ref, sq_scr, sem.at[0]),
        pltpu.make_async_copy(dec_q_ref, dq_scr, sem.at[1]),
        pltpu.make_async_copy(new_k_ref.at[:, :, lanes], nk_scr, sem.at[2]),
        pltpu.make_async_copy(new_v_ref.at[:, :, lanes], nv_scr, sem.at[3]),
        pltpu.make_async_copy(gen_k_ref.at[:, :, lanes], gk_scr, sem.at[4]),
        pltpu.make_async_copy(gen_v_ref.at[:, :, lanes], gv_scr, sem.at[5]),
    ]
    for copy in copies:
        copy.start()

    me = lax.axis_index("seq")
    base_rows = prompts * shards
    count = table_ref.shape[1]
    position = iota((count, HEAD_WIDTH), 0)
    for p in range(prompts):
        start = ch + p * shards
        row = iota((count, HEAD_WIDTH), 0)
        here = (row >= start) & (row < start + shards)
        position = jnp.where(here, begin_ref[p] + (row - start) * ch, position)
    for r in range(rows_local):
        start = ch + base_rows + r * steps
        row = iota((count, HEAD_WIDTH), 0)
        here = (row >= start) & (row < start + steps)
        length = begin_ref[request_ref[r]] + ch * shards + length_ref[r]
        position = jnp.where(here, length + row - start, position)
    cosine, sine = angle_tables(position)
    table_ref[0] = cosine
    table_ref[1] = sine

    copies[0].wait()
    for p in range(prompts):
        cosine, sine = token_tables(table_ref, ch, ch + p * shards + me)
        for h in range(used):
            for g in range(per_kv):
                x = sq_scr[p, :, tile(h * per_kv + g)].astype(f32)
                q_ref[p, h, pl.ds(g * ch, ch), :] = rotate(x, cosine, sine).astype(bf16)

    for copy in copies[1:4]:
        copy.wait()
    n_scr[...] = jnp.zeros_like(n_scr)
    pad = n_scr.shape[2]
    for r in range(rows_local):
        rows = pl.ds(ch + base_rows + r * steps, steps)
        cosine = table_ref[0, rows, :]
        sine = signed(table_ref[1, rows, :])
        for h in range(used):
            for g in range(per_kv):
                x = dq_scr[r, :, tile(h * per_kv + g)].astype(f32)
                q_scr[h, pl.ds(r * step_rows + g * steps, steps), :] = rotate(x, cosine, sine)
            n_scr[0, r * used + h, pl.ds(0, steps), :] = rotate(
                nk_scr[r, :, tile(h)].astype(f32), cosine, sine
            )
            n_scr[1, r * used + h, pl.ds(0, steps), :] = nv_scr[r, :, tile(h)].astype(f32)

    for h in range(used):
        for r in range(rows_local):
            rows = pl.ds(r * step_rows, step_rows)
            x = q_scr[h, rows, :]
            for p in range(prompts):
                q_cat_ref[h, rows, tile(p)] = jnp.where(request_ref[r] == p, x, 0.0).astype(bf16)

    for copy in copies[4:]:
        copy.wait()
    span = min(HEAD_WIDTH, dec_rows)
    group = span // step_rows
    lengths = by_row(length_ref, dec_rows, step_rows)
    begins = by_row(request_ref, dec_rows, step_rows, begin_ref)
    requests = by_row(request_ref, dec_rows, step_rows)
    key = iota((gen + pad, span), 0)
    lane = iota((gen + pad, span), 1)
    new_seen = (key >= gen) & (key - gen <= lane % steps)
    for h in range(used):
        stat_ref[h, pl.ds(2, 1), :] = begins.astype(f32)
        stat_ref[h, pl.ds(3, 1), :] = requests.astype(f32)
        for i in range(dec_rows // span):
            cols = pl.ds(i * span, span)
            q = q_scr[h, cols, :].astype(bf16)
            row = iota((span, HEAD_WIDTH), 0) // step_rows
            scores = None
            for j in range(group):
                r = i * group + j
                keys = jnp.concatenate(
                    [gk_scr[r, :, tile(h)], n_scr[0, r * used + h].astype(bf16)], axis=0
                )
                part = dot_nt(keys, jnp.where(row == j, q, jnp.zeros_like(q)))
                scores = part if scores is None else scores + part
            seen = (key < lengths[:, i * span : (i + 1) * span]) | new_seen
            scores = jnp.where(seen, scores, very_low)
            top = jnp.max(scores, axis=0, keepdims=True)
            weights = jnp.exp2((scores - top) * RATE)
            total = jnp.sum(weights, axis=0, keepdims=True)
            acc = None
            for j in range(group):
                r = i * group + j
                values = jnp.concatenate(
                    [gv_scr[r, :, tile(h)], n_scr[1, r * used + h].astype(bf16)], axis=0
                )
                part = dot_tn(
                    values, jnp.where(lane // step_rows == j, weights, 0.0).astype(bf16)
                )
                acc = part if acc is None else acc + part
            acc_ref[h, :, cols] = acc
            stat_ref[h, pl.ds(0, 1), cols] = top
            stat_ref[h, pl.ds(1, 1), cols] = total


def rotate_keys(chunk_ref, k_scr, table_ref, shards, prompts, used, pre, ch, shard, at):
    k_scr[pl.ds(at, pre), :] = chunk_ref[pl.ds(0, pre), :]
    for p in range(prompts):
        cosine, sine = token_tables(table_ref, ch, ch + p * shards + shard)
        for h in range(used):
            lanes = tile(h * prompts + p)
            x = chunk_ref[pl.ds(pre, ch), lanes].astype(f32)
            k_scr[pl.ds(at + pre, ch), lanes] = rotate(x, cosine, sine).astype(bf16)


def hide(scores, pre, begin, last):
    low = scores[:pre]
    low = jnp.where(iota(low.shape, 0) < begin, low, very_low)
    high = scores[pre:]
    if last is not None:
        high = jnp.where(iota(high.shape, 0) <= last, high, very_low)
    return jnp.concatenate([low, high], axis=0)


def masked_stack(weights, requests, prompts):
    return jnp.concatenate(
        [jnp.where(requests == p, weights, 0.0).astype(bf16) for p in range(prompts)], axis=0
    )


def near_kernel(shards, used, ch, hops, *refs):
    count = len(hops)
    begin_ref = refs[0]
    keys, values = refs[1 : 1 + count], refs[1 + count : 1 + 2 * count]
    table_ref, q_ref, q_cat_ref, acc_in_ref, stat_in_ref = refs[1 + 2 * count : 6 + 2 * count]
    before = refs[6 + 2 * count : -5]
    acc_ref, stat_ref, dec_acc_ref, dec_stat_ref, k_scr = refs[-5:]
    prompts, _, rows, _ = q_ref.shape
    size = keys[0].shape[0]
    me = lax.axis_index("seq")
    pre = size - ch
    shard = [ring_source(me, shards, hop) for hop in hops]
    for c in range(count):
        rotate_keys(
            keys[c], k_scr, table_ref, shards, prompts, used, pre, ch, shard[c], c * size
        )
    token = me * ch + iota((1, rows), 1) % ch
    for h in range(used):
        requests = stat_in_ref[h, pl.ds(3, 1), :]
        begins = stat_in_ref[h, pl.ds(2, 1), :].astype(jnp.int32)
        for p in range(prompts):
            pieces = []
            for c in range(count):
                k = k_scr[pl.ds(c * size, size), tile(h * prompts + p)]
                pieces.append(
                    hide(
                        dot_nt(k, q_ref[p, h]),
                        pre,
                        begin_ref[p] - shard[c] * pre,
                        token - shard[c] * ch,
                    )
                )
            scores = jnp.concatenate(pieces, axis=0)
            top = jnp.max(scores, axis=0, keepdims=True)
            if before:
                old_top = before[1][p, h, pl.ds(0, 1), :]
                top = jnp.maximum(top, old_top)
            weights = jnp.exp2((scores - top) * RATE)
            total = jnp.sum(weights, axis=0, keepdims=True)
            v = jnp.concatenate(
                [ref[pl.ds(p * size, size), tile(h)] for ref in values], axis=0
            )
            acc = dot_tn(v, weights.astype(bf16))
            if before:
                factor = jnp.exp2((old_top - top) * RATE)
                total = total + before[1][p, h, pl.ds(1, 1), :] * factor
                acc = acc + before[0][p, h] * factor
            acc_ref[p, h] = acc
            stat_ref[p, h, pl.ds(0, 1), :] = top
            stat_ref[p, h, pl.ds(1, 1), :] = total

        pieces = []
        for c in range(count):
            k = k_scr[pl.ds(c * size, size), pl.ds(h * prompts * HEAD_WIDTH, prompts * HEAD_WIDTH)]
            pieces.append(hide(dot_nt(k, q_cat_ref[h]), pre, begins - shard[c] * pre, None))
        scores = jnp.concatenate(pieces, axis=0)
        old_top = stat_in_ref[h, pl.ds(0, 1), :]
        top = jnp.maximum(jnp.max(scores, axis=0, keepdims=True), old_top)
        factor = jnp.exp2((old_top - top) * RATE)
        weights = jnp.exp2((scores - top) * RATE)
        total = jnp.sum(weights, axis=0, keepdims=True) + stat_in_ref[h, pl.ds(1, 1), :] * factor
        acc = acc_in_ref[h] * factor
        for c in range(count):
            w = masked_stack(weights[c * size : (c + 1) * size], requests, prompts)
            acc = acc + dot_tn(values[c][:, tile(h)], w)
        dec_acc_ref[h] = acc
        dec_stat_ref[h, pl.ds(0, 1), :] = top
        dec_stat_ref[h, pl.ds(1, 1), :] = total
        dec_stat_ref[h, pl.ds(2, 2), :] = stat_in_ref[h, pl.ds(2, 2), :]


def far_kernel(
    shards,
    used,
    ch,
    begin_ref,
    key_ref,
    table_ref,
    q_ref,
    q_cat_ref,
    acc_ref,
    stat_ref,
    dec_acc_ref,
    dec_stat_ref,
    base_ref,
    weight_ref,
    dec_base_ref,
    dec_weight_ref,
    k_scr,
):
    prompts, _, rows, _ = q_ref.shape
    size = key_ref.shape[0]
    me = lax.axis_index("seq")
    pre = size - ch
    shard = ring_source(me, shards, shards - 1)
    rotate_keys(key_ref, k_scr, table_ref, shards, prompts, used, pre, ch, shard, 0)
    token = me * ch + iota((1, rows), 1) % ch

    def finish(scores, old_top, old_total, old_acc):
        top = jnp.maximum(jnp.max(scores, axis=0, keepdims=True), old_top)
        factor = jnp.exp2((old_top - top) * RATE)
        weights = jnp.exp2((scores - top) * RATE)
        total = jnp.sum(weights, axis=0, keepdims=True) + old_total * factor
        inverse = 1.0 / total
        return weights * inverse, old_acc * (factor * inverse)

    for h in range(used):
        for p in range(prompts):
            scores = hide(
                dot_nt(k_scr[:, tile(h * prompts + p)], q_ref[p, h]),
                pre,
                begin_ref[p] - shard * pre,
                token - shard * ch,
            )
            weights, base = finish(
                scores, stat_ref[p, h, pl.ds(0, 1), :], stat_ref[p, h, pl.ds(1, 1), :], acc_ref[p, h]
            )
            weight_ref[p, h] = weights.T.astype(bf16)
            base_ref[p, h] = base.T
        begins = dec_stat_ref[h, pl.ds(2, 1), :].astype(jnp.int32)
        requests = dec_stat_ref[h, pl.ds(3, 1), :]
        k = k_scr[:, pl.ds(h * prompts * HEAD_WIDTH, prompts * HEAD_WIDTH)]
        scores = hide(dot_nt(k, q_cat_ref[h]), pre, begins - shard * pre, None)
        weights, base = finish(
            scores, dec_stat_ref[h, pl.ds(0, 1), :], dec_stat_ref[h, pl.ds(1, 1), :], dec_acc_ref[h]
        )
        stack = jnp.concatenate(
            [jnp.where(requests == p, weights, 0.0) for p in range(prompts)], axis=0
        )
        dec_weight_ref[h] = stack.T.astype(bf16)
        dec_base_ref[h] = base.T


def last_kernel(
    used,
    per_kv,
    steps,
    value_ref,
    base_ref,
    weight_ref,
    dec_base_ref,
    dec_weight_ref,
    span_ref,
    dec_ref,
    span_scr,
    dec_scr,
    sem,
):
    prompts, _, rows, size = weight_ref.shape
    ch = rows // per_kv
    step_rows = per_kv * steps
    copies = []
    for p in range(prompts):
        for h in range(used):
            out = base_ref[p, h] + jnp.dot(
                weight_ref[p, h],
                value_ref[pl.ds(p * size, size), tile(h)],
                preferred_element_type=f32,
            )
            out = out.astype(bf16)
            for g in range(per_kv):
                span_scr[p, :, tile(h * per_kv + g)] = out[g * ch : (g + 1) * ch]
        copies.append(pltpu.make_async_copy(span_scr.at[p], span_ref.at[p], sem.at[p]))
        copies[-1].start()
    for h in range(used):
        out = dec_base_ref[h] + jnp.dot(
            dec_weight_ref[h], value_ref[:, tile(h)], preferred_element_type=f32
        )
        for r in range(dec_scr.shape[0]):
            for g in range(per_kv):
                start = r * step_rows + g * steps
                dec_scr[r, :, tile(h * per_kv + g)] = out[start : start + steps].astype(bf16)
    copies.append(pltpu.make_async_copy(dec_scr, dec_ref, sem.at[prompts]))
    copies[-1].start()
    for copy in copies:
        copy.wait()


def body(
    span_q,
    span_raw_keys,
    span_raw_values,
    prompt_cache_keys,
    prompt_cache_values,
    span_offsets,
    decode_new_queries,
    decode_new_keys,
    decode_new_values,
    generated_keys,
    generated_values,
    row_request,
    row_length,
):
    prompts, ch, q_width = span_q.shape
    pre = prompt_cache_keys.shape[1]
    q_heads = q_width // HEAD_WIDTH
    kv_local = span_raw_keys.shape[2] // HEAD_WIDTH
    used = max(1, q_heads // GROUPS)
    per_kv = q_heads // used
    width = used * HEAD_WIDTH
    shards = lax.axis_size("seq")
    rows_local, steps = decode_new_queries.shape[:2]
    gen = generated_keys.shape[1]
    step_rows = per_kv * steps
    dec_rows = rows_local * step_rows
    rows = per_kv * ch
    size = pre + ch
    params = functools.partial(pltpu.CompilerParams, vmem_limit_bytes=16 << 20)
    shape = jax.ShapeDtypeStruct

    own_keys = pl.pallas_call(
        functools.partial(pack_keys_kernel, q_heads, kv_local, used),
        out_shape=shape((size, prompts * width), bf16),
        in_specs=[HBM, HBM],
        out_specs=VMEM,
        scratch_shapes=[pltpu.SemaphoreType.DMA((prompts, used, 2))],
        compiler_params=params(),
        cost_estimate=cost(1),
        name="pack_keys",
    )(*in_hbm(prompt_cache_keys, span_raw_keys))
    own_values = pl.pallas_call(
        functools.partial(pack_values_kernel, q_heads, kv_local, used),
        out_shape=shape((prompts * size, width), bf16),
        in_specs=[HBM, HBM, ANY],
        out_specs=VMEM,
        scratch_shapes=[pltpu.SemaphoreType.DMA((prompts, 2))],
        compiler_params=params(),
        cost_estimate=cost(1),
        name="pack_values",
    )(*in_hbm(prompt_cache_values, span_raw_values), own_keys)

    order = ring_order(shards)
    ring = list(zip(order, order[1:] + order[:1]))
    keys = [own_keys]
    values = [own_values]
    for _ in range(1, shards):
        keys.append(lax.ppermute(keys[-1], "seq", ring))
        values.append(lax.ppermute(values[-1], "seq", ring))

    table_rows = -(-(ch + prompts * shards + rows_local * steps) // 8) * 8
    table, queries, dec_queries, gen_acc, gen_stat = pl.pallas_call(
        functools.partial(prepare_kernel, shards, q_heads, kv_local, used, per_kv),
        out_shape=[
            shape((2, table_rows, HEAD_WIDTH), f32),
            shape((prompts, used, rows, HEAD_WIDTH), bf16),
            shape((used, dec_rows, prompts * HEAD_WIDTH), bf16),
            shape((used, HEAD_WIDTH, dec_rows), f32),
            shape((used, 8, dec_rows), f32),
        ],
        in_specs=[SMEM] * 3 + [HBM] * 6,
        out_specs=[VMEM] * 5,
        scratch_shapes=[
            pltpu.VMEM(span_q.shape, bf16),
            pltpu.VMEM(decode_new_queries.shape, bf16),
            pltpu.VMEM((rows_local, steps, width), bf16),
            pltpu.VMEM((rows_local, steps, width), bf16),
            pltpu.VMEM((rows_local, gen, width), bf16),
            pltpu.VMEM((rows_local, gen, width), bf16),
            pltpu.VMEM((used, dec_rows, HEAD_WIDTH), f32),
            pltpu.VMEM((2, rows_local * used, 16, HEAD_WIDTH), f32),
            pltpu.SemaphoreType.DMA((6,)),
        ],
        compiler_params=params(),
        cost_estimate=cost(3),
        name="prepare",
    )(
        span_offsets,
        row_request,
        row_length,
        *in_hbm(
            span_q,
            decode_new_queries,
            decode_new_keys,
            decode_new_values,
            generated_keys,
            generated_values,
        ),
    )

    prompt_state = [
        shape((prompts, used, HEAD_WIDTH, rows), f32),
        shape((prompts, used, 8, rows), f32),
    ]
    row_state = [shape((used, HEAD_WIDTH, dec_rows), f32), shape((used, 8, dec_rows), f32)]
    near = [gen_acc, gen_stat]
    for step in range(1, max(2, shards - 1)):
        hops = [hop for hop in ([0, 1] if step == 1 else [step]) if hop < shards - 1]
        ins = [span_offsets, *[keys[hop] for hop in hops], *[values[hop] for hop in hops]]
        ins += [table, queries, dec_queries, *near[-2:], *near[:-2]]
        near = pl.pallas_call(
            functools.partial(near_kernel, shards, used, ch, hops),
            out_shape=prompt_state + row_state,
            in_specs=[SMEM] + [VMEM] * (len(ins) - 1),
            out_specs=[VMEM] * 4,
            scratch_shapes=[pltpu.VMEM((len(hops) * size, prompts * width), bf16)],
            compiler_params=params(),
            cost_estimate=cost(3),
        )(*ins)

    far = pl.pallas_call(
        functools.partial(far_kernel, shards, used, ch),
        out_shape=[
            shape((prompts, used, rows, HEAD_WIDTH), f32),
            shape((prompts, used, rows, size), bf16),
            shape((used, dec_rows, HEAD_WIDTH), f32),
            shape((used, dec_rows, prompts * size), bf16),
        ],
        in_specs=[SMEM] + [VMEM] * 8,
        out_specs=[VMEM] * 4,
        scratch_shapes=[pltpu.VMEM((size, prompts * width), bf16)],
        compiler_params=params(),
        cost_estimate=cost(2),
        name="far",
    )(span_offsets, keys[-1], table, queries, dec_queries, *near)

    return tuple(
        pl.pallas_call(
            functools.partial(last_kernel, used, per_kv, steps),
            out_shape=[
                shape(span_q.shape, bf16),
                shape(decode_new_queries.shape, bf16),
            ],
            in_specs=[VMEM] * 5,
            out_specs=[HBM, HBM],
            scratch_shapes=[
                pltpu.VMEM(span_q.shape, bf16),
                pltpu.VMEM(decode_new_queries.shape, bf16),
                pltpu.SemaphoreType.DMA((prompts + 1,)),
            ],
            compiler_params=params(),
            cost_estimate=cost(1),
        name="last",
        )(values[-1], *far)
    )


def solution(mesh):
    in_specs = (
        P("group", "seq", ("head", "rep")),
        P("group", "seq", "head"),
        P("group", "seq", "head"),
        P("group", "seq", "head"),
        P("group", "seq", "head"),
        P("group"),
        P(("group", "seq"), None, ("head", "rep")),
        P(("group", "seq"), None, "head"),
        P(("group", "seq"), None, "head"),
        P(("group", "seq"), None, "head"),
        P(("group", "seq"), None, "head"),
        P(("group", "seq")),
        P(("group", "seq")),
    )
    out_specs = (P("group", "seq", ("head", "rep")), P(("group", "seq"), None, ("head", "rep")))
    return jax.shard_map(body, mesh=mesh, in_specs=in_specs, out_specs=out_specs, check_vma=False)
```
